32 devices in a mesh: groups: 2 (over y), expert: 4 (over x, core), replica: 4 (over z).
Axes of the slice: x: 2, y: 2, z: 4, core: 2. Of those that a mesh axis runs over, the one named last changes fastest.
Arguments:
- tokens: bfloat16 [8192, 2048], P(('groups', 'expert', 'replica')), parts along dimension 0, may hold values from -6 to 6
- norm_gain: float32 [2048], replicated, may hold values from 0.1 to 1.9
- router: bfloat16 [2048, 16], replicated, may hold values from -0.125 to 0.125
- down_proj: bfloat16 [2048, 512], P(('expert', 'replica')), may hold values from -0.125 to 0.125
- up_proj: bfloat16 [2048, 512], P(('expert', 'replica')), may hold values from -0.25 to 0.25
- expert_gate: bfloat16 [16, 512, 768], P('expert'), may hold values from -0.25 to 0.25
- expert_up: bfloat16 [16, 512, 768], P('expert'), may hold values from -0.25 to 0.25
- expert_down: bfloat16 [16, 768, 512], P('expert'), may hold values from -0.21875 to 0.21875
- expert_ids: int32 [8192, 8], P(('groups', 'expert', 'replica')), parts along dimension 0, may hold values from 0 to 15, as said below
- slot_pos: int32 [8192, 8], P(('groups', 'expert', 'replica')), parts along dimension 0, may hold values from -1 to 127, as said below
- overflow_list: int32 [32, 4, 4, 4], P(('groups', 'expert', 'replica')), parts along dimension 0, may hold values from -1 to 2047, as said below
Outputs:
- mixed: bfloat16 [8192, 2048], P(('groups', 'expert', 'replica')), parts along dimension 0
The draws below stay inside these ranges and needn't reach their ends.
There are 2 independent parts, one for each index of `groups`. The reference program is written for one: setup_inputs(seed, part) draws one part's arguments, and reference() takes and returns one part's arrays. A program takes and returns all parts, laid end to end along the dimension named above; an argument that names none is the same for every part. Nothing has to cross between parts.
Inputs may be any that keep to these rules, and one draw needn't show every extreme that they name: `expert_ids`: the 8 ids of a token are distinct. `slot_pos`: within the 256 rows of one device, the choices of one expert that have a slot hold distinct slots 0, 1, 2, ... in row order, so at most 128 from one device to one expert; in every draw some expert gets all 128 slots from every device. `overflow_list`: an entry is a choice index t' * 8 + k of the source device's own rows whose expert is (destination index of the expert axis) * 4 + (local expert) and whose slot_pos is -1; each choice is listed at most once. In every draw some expert is listed at every copy by every source device.
All inputs are finite; a program needn't handle non-finite values.
Results may differ from the reference program's by a relative error of at most 0.0088.
Values may be sent and summed in bfloat16 or wider, within the bound.
No kernel may reach another device: no remote copies, remote signals or barrier semaphores. Data moves between devices by JAX's collectives and lax.ppermute only.
A program may use at most 128 MiB of HBM per device.

```python
import jax
import jax.numpy as jnp
from jax import lax

D = 2048
LATENT = 512
EXPERT_FF = 768
TOPK = 8
EXP_DEV = 4
TOK_DEV = 256
EXPERT_SHARDS = 4
COPIES = 4
SOURCES = 16
SPECIALIST_COUNT = 16
CAP = 128
TOKENS = 4096


def place_entries(table, cells, entries):
    return table.at[cells].set(entries, mode='drop')


def routing_tables(key):
    base = jax.random.fold_in(key, 11)
    k_hot, k_pop, k_noise, k_shift = jax.random.split(base, 4)
    busiest_specialist = jax.random.randint(k_hot, (), 0, SPECIALIST_COUNT)
    favored_specialist = jax.random.randint(k_pop, (SPECIALIST_COUNT,), 0, 4 * SPECIALIST_COUNT)
    gating_jitter = jax.random.randint(k_noise, (SOURCES, TOK_DEV, SPECIALIST_COUNT), 0, 8 * SPECIALIST_COUNT)
    shifts = jax.random.randint(k_shift, (SOURCES, 1), 0, TOK_DEV)
    places = jnp.arange(TOK_DEV, dtype=jnp.int32)[None, :]
    imposed_selection = (places + shifts) % TOK_DEV < CAP + COPIES
    feature_band = jnp.arange(SPECIALIST_COUNT, dtype=jnp.int32)
    extra_preference = jnp.where(imposed_selection[:, :, None] & (feature_band == busiest_specialist)[None, None, :], 16 * SPECIALIST_COUNT, 0)
    gating_affinity = (favored_specialist[None, None, :] + gating_jitter + extra_preference) * SPECIALIST_COUNT + feature_band
    _, chosen = lax.top_k(gating_affinity, TOPK)
    chosen = chosen.astype(jnp.int32)
    flat = chosen.reshape(SOURCES, TOK_DEV * TOPK)
    onehot = (flat[:, :, None] == feature_band[None, None, :]).astype(jnp.int32)
    before = jnp.cumsum(onehot, axis=1) - onehot
    rank = jnp.sum(before * onehot, axis=2)
    slots = jnp.where(rank < CAP, rank, -1).astype(jnp.int32)
    spill = rank - CAP
    owner = (jnp.arange(SOURCES, dtype=jnp.int32) % COPIES)[:, None]
    target = (owner + 1 + spill) % COPIES
    valid = (spill >= 0) & (spill < COPIES)
    cells = jnp.where(valid, flat * COPIES + target, SPECIALIST_COUNT * COPIES).astype(jnp.int32)
    entries = jnp.broadcast_to(jnp.arange(TOK_DEV * TOPK, dtype=jnp.int32)[None, :], flat.shape)
    table = jnp.full((SOURCES, SPECIALIST_COUNT * COPIES), -1, jnp.int32)
    table = jax.vmap(place_entries)(table, cells, entries)
    table = table.reshape(SOURCES, EXPERT_SHARDS, EXP_DEV, COPIES).transpose(0, 1, 3, 2)
    return (chosen.reshape(TOKENS, TOPK), slots.reshape(TOKENS, TOPK), table)


def draw_expert_ids(key, part):
    return routing_tables(key)[0]


def draw_slot_pos(key, part):
    return routing_tables(key)[1]


def draw_overflow_list(key, part):
    return routing_tables(key)[2]


def shard_levels(own_key, extent, shards, smallest, largest):
    def one(axis_at, blocks):
        draws = jax.random.uniform(jax.random.fold_in(jax.random.fold_in(own_key, 6), axis_at), (blocks,), jnp.float32, smallest / len(shards), largest / len(shards))
        return jnp.repeat(jnp.exp(draws), extent[axis_at] // blocks).reshape((-1,) + (1,) * (len(extent) - axis_at - 1))

    gain = one(*shards[0])
    for cut in shards[1:]:
        gain = gain * one(*cut)
    return gain


def normal_values(rng, extent, width, limit, pieces=(), kind=jnp.bfloat16):
    values = width * jax.random.normal(rng, extent, jnp.float32)
    if pieces:
        values = values * shard_levels(rng, extent, pieces, -0.22, 0.18)
    return jnp.clip(values, -limit, limit).astype(kind)


def setup_inputs(seed: int = 0, part: int = 0) -> dict:
    key_of = jax.random.split(jax.random.key(seed), 12)
    own_keys = jax.random.split(jax.random.fold_in(key_of[11], part), 12)
    tokens = normal_values(own_keys[0], (TOKENS, D), 1.0, 6.0, ((0, 16),))
    norm_gain = jnp.clip(1.0 + 0.18 * jax.random.normal(key_of[1], (D,), jnp.float32), 0.1, 1.9)
    router = normal_values(key_of[2], (D, SPECIALIST_COUNT), D ** -0.5, 0.125)
    down_proj = normal_values(key_of[3], (D, LATENT), D ** -0.5, 0.125, ((0, 16),))
    up_proj = normal_values(key_of[4], (D, LATENT), LATENT ** -0.5, 0.25, ((0, 16),))
    expert_gate = normal_values(key_of[5], (SPECIALIST_COUNT, LATENT, EXPERT_FF), LATENT ** -0.5, 0.25, ((0, 4),))
    expert_up = normal_values(key_of[6], (SPECIALIST_COUNT, LATENT, EXPERT_FF), LATENT ** -0.5, 0.25, ((0, 4),))
    expert_down = normal_values(key_of[7], (SPECIALIST_COUNT, EXPERT_FF, LATENT), EXPERT_FF ** -0.5, 0.21875, ((0, 4),))
    expert_ids = draw_expert_ids(jax.random.fold_in(jax.random.fold_in(key_of[11], part), 71), part)
    slot_pos = draw_slot_pos(jax.random.fold_in(jax.random.fold_in(key_of[11], part), 71), part)
    overflow_list = draw_overflow_list(jax.random.fold_in(jax.random.fold_in(key_of[11], part), 71), part)
    return dict(tokens=tokens, norm_gain=norm_gain, router=router, down_proj=down_proj, up_proj=up_proj, expert_gate=expert_gate, expert_up=expert_up, expert_down=expert_down, expert_ids=expert_ids, slot_pos=slot_pos, overflow_list=overflow_list)


epsilon = 1e-06

def reference(tokens, norm_gain, router, down_proj, up_proj, expert_gate, expert_up, expert_down, expert_ids, slot_pos, overflow_list):
    values = tokens.astype(jnp.float32)
    scaled = values * lax.rsqrt(lax.optimization_barrier(jnp.mean(values * values, axis=-1, keepdims=True)) + epsilon)
    normed = (scaled * norm_gain).astype(jnp.bfloat16)
    latent = jnp.dot(normed, down_proj, preferred_element_type=jnp.float32).astype(jnp.bfloat16)
    logits = jnp.dot(normed, router, preferred_element_type=jnp.float32)
    chosen = jnp.take_along_axis(logits, expert_ids, axis=1)
    sigmas = jax.nn.sigmoid(chosen)
    gates = (sigmas / lax.optimization_barrier(jnp.sum(sigmas, axis=1, keepdims=True))).reshape(-1)
    per_source = TOK_DEV * TOPK
    assign = jnp.arange(TOKENS * TOPK, dtype=jnp.int32)
    source = assign // per_source
    flat_ids = expert_ids.reshape(-1).astype(jnp.int32)
    flat_pos = slot_pos.reshape(-1).astype(jnp.int32)
    slot_index = jnp.where(flat_pos >= 0, (source * SPECIALIST_COUNT + flat_ids) * CAP + flat_pos, SOURCES * SPECIALIST_COUNT * CAP)
    first_list = jnp.full((SOURCES * SPECIALIST_COUNT * CAP,), -1, jnp.int32).at[slot_index].set(assign, mode='drop')
    first_list = first_list.reshape(SOURCES, SPECIALIST_COUNT, CAP).transpose(1, 0, 2).reshape(SPECIALIST_COUNT, SOURCES * CAP)
    offsets = (jnp.arange(SOURCES, dtype=jnp.int32) * per_source)[:, None, None, None]
    spare_list = jnp.where(overflow_list >= 0, overflow_list + offsets, -1).astype(jnp.int32)
    spare_list = spare_list.transpose(1, 3, 0, 2).reshape(SPECIALIST_COUNT, SOURCES * COPIES)
    row_lists = jnp.concatenate([first_list, spare_list], axis=1)

    def expert_step(combined, inputs):
        entries, w_gate, w_up, w_down = inputs
        valid = entries >= 0
        safe = jnp.maximum(entries, 0)
        rows = latent[safe // TOPK]
        gate = jnp.dot(rows, w_gate, preferred_element_type=jnp.float32)
        upper = jnp.dot(rows, w_up, preferred_element_type=jnp.float32)
        hidden = (jax.nn.silu(gate) * upper).astype(jnp.bfloat16)
        result = jnp.dot(hidden, w_down, preferred_element_type=jnp.float32).astype(jnp.bfloat16)
        weight = jnp.where(valid, gates[safe], jnp.zeros((), jnp.float32))
        combined = combined.at[safe // TOPK].add(result.astype(jnp.float32) * weight[:, None])
        return (combined, None)
    start = jnp.zeros((TOKENS, LATENT), jnp.float32)
    combined, _ = lax.scan(expert_step, start, (row_lists, expert_gate, expert_up, expert_down))
    merged = combined.astype(jnp.bfloat16)
    output = lax.dot_general(merged, up_proj, (((1,), (1,)), ((), ())), preferred_element_type=jnp.float32)
    return output.astype(jnp.bfloat16)
```

```python
import functools

import jax
import jax.numpy as jnp
from jax import lax
from jax.experimental import pallas as pl
from jax.experimental.pallas import tpu as pltpu
from jax.sharding import PartitionSpec as P

epsilon = 1e-06
F32 = jnp.float32
BF16 = jnp.bfloat16

VM = pl.BlockSpec(memory_space=pltpu.VMEM)
SM = pl.BlockSpec(memory_space=pltpu.SMEM)


def swap(x, axis, bits):
    size = lax.axis_size(axis)
    return lax.ppermute(x, axis, [(i, i ^ bits) for i in range(size)])


def grant(mib):
    return pltpu.CompilerParams(vmem_limit_bytes=mib * 1024 * 1024)


def cost(flops, nbytes):
    return pl.CostEstimate(flops=flops, bytes_accessed=nbytes, transcendentals=0)


def gate_kernel(top, wide, pos_ref, tok_ref, gain_ref, router_ref, ids_ref, slot_ref, list_ref,
                keep_ref, send_ref, wt_ref, normed_ref):
    values = tok_ref[...].astype(F32)
    scale = lax.rsqrt(jnp.mean(values * values, axis=-1, keepdims=True) + epsilon)
    normed = (values * scale * gain_ref[...]).astype(BF16)
    normed_ref[...] = normed
    core = pos_ref[0]
    for h in range(keep_ref.shape[1] // wide):
        mine = pl.multiple_of((2 * h + core) * wide, wide)
        other = pl.multiple_of((2 * h + 1 - core) * wide, wide)
        keep_ref[:, h * wide:(h + 1) * wide] = normed_ref[:, pl.ds(mine, wide)]
        send_ref[:, h * wide:(h + 1) * wide] = normed_ref[:, pl.ds(other, wide)]
    sig = jax.nn.sigmoid(jnp.dot(normed, router_ref[...], preferred_element_type=F32))
    rows, experts = sig.shape
    lane = lax.broadcasted_iota(jnp.int32, (rows, experts), 1)
    row = lax.broadcasted_iota(jnp.int32, (rows, experts), 0)
    ids = ids_ref[...]
    slot = slot_ref[...]
    total = jnp.zeros((rows, experts), F32)
    served = jnp.zeros((rows, experts), F32)
    for k in range(top):
        hit = lane == ids[:, k:k + 1]
        total = total + jnp.where(hit, 1.0, 0.0)
        served = served + jnp.where(hit & (slot[:, k:k + 1] >= 0), 1.0, 0.0)
    for q in range(list_ref.shape[0]):
        entry = list_ref[q:q + 1, :]
        owner = jnp.where(entry >= 0, entry, -top) // top
        served = served + jnp.where(row == owner, 1.0, 0.0)
    denom = jnp.sum(total * sig, axis=1, keepdims=True)
    weight = jnp.where(served > 0.0, sig / denom, 0.0)
    pad = jnp.zeros((rows, 128 - experts), F32)
    wt_ref[...] = jnp.concatenate([weight, pad], axis=1).T[:experts, :]


def latent_kernel(chunks, wide, pos_ref, keep_ref, recv_ref, *refs):
    out_ref = refs[-1]
    half, rep = pos_ref[1], pos_ref[2]
    rows = keep_ref.shape[0]
    acc = [jnp.zeros((rows, out_ref.shape[1]), F32) for _ in range(2)]
    for (a, b), w_ref in zip(chunks, refs[:-1]):
        depth = w_ref.shape[0]
        at = pl.multiple_of((half ^ a) * wide + (rep ^ b) * depth, depth)
        w = w_ref[...]
        for i, x_ref in enumerate((keep_ref, recv_ref)):
            acc[i] += jnp.dot(x_ref[:, pl.ds(at, depth)], w, preferred_element_type=F32)
    out_ref[:rows, :] = acc[0]
    out_ref[rows:, :] = acc[1]


def finish_kernel(mine_ref, recv_ref, own_ref, core_ref):
    rows = own_ref.shape[0]
    own_ref[...] = (mine_ref[:rows, :] + recv_ref[rows:, :]).astype(BF16)
    core_ref[...] = (mine_ref[rows:, :] + recv_ref[:rows, :]).astype(BF16)


def expert_kernel(local, pos_ref, x0_ref, x1_ref, w0_ref, w1_ref, g_ref, u_ref, d_ref, o0_ref, o1_ref,
                  acc_ref, col_ref):
    j = pl.program_id(0)
    rows = x0_ref.shape[0]
    me = pos_ref[3]

    @pl.when(j == 0)
    def _():
        acc_ref[...] = jnp.zeros_like(acc_ref)
        for i, w_ref in enumerate((w0_ref, w1_ref)):
            wt = w_ref[...]
            pad = jnp.zeros((128 - wt.shape[0], rows), F32)
            col_ref[i * rows:(i + 1) * rows, :] = jnp.concatenate([wt, pad], axis=0).T

    for i, x_ref in enumerate((x0_ref, x1_ref)):
        x = x_ref[...]
        gate = jnp.dot(x, g_ref[0], preferred_element_type=F32)
        upper = jnp.dot(x, u_ref[0], preferred_element_type=F32)
        half = 0.5 * gate
        hidden = ((half + half * jnp.tanh(half)) * upper).astype(BF16)
        result = jnp.dot(hidden, d_ref[0], preferred_element_type=F32).astype(BF16).astype(F32)
        cols = col_ref[i * rows:(i + 1) * rows, :]
        lane = lax.broadcasted_iota(jnp.int32, cols.shape, 1)
        weight = jnp.sum(jnp.where(lane == me * local + j, cols, 0.0), axis=1, keepdims=True)
        acc_ref[i * rows:(i + 1) * rows, :] += result * weight

    @pl.when(j == local - 1)
    def _():
        o0_ref[...] = acc_ref[:rows, :].astype(BF16)
        o1_ref[...] = acc_ref[rows:, :].astype(BF16)


def add_kernel(a_ref, b_ref, o_ref):
    o_ref[...] = (a_ref[...].astype(F32) + b_ref[...].astype(F32)).astype(BF16)


def final_kernel(n_sum, chunks, copies, depth, pos_ref, *refs):
    out_ref = refs[-1]
    half, rep, core = pos_ref[1], pos_ref[2], pos_ref[0]
    total = refs[0][...].astype(F32)
    for s_ref in refs[1:n_sum]:
        total = total + s_ref[...].astype(F32)
    merged = total.astype(BF16)
    for (c, b), w_ref in zip(chunks, refs[n_sum:-1]):
        for a in range(w_ref.shape[0] // depth):
            e = 2 * (half ^ a) + (core ^ c)
            at = pl.multiple_of((e * copies + (rep ^ b)) * depth, depth)
            out_ref[:, pl.ds(at, depth)] = lax.dot_general(
                merged, w_ref[a * depth:(a + 1) * depth, :], (((1,), (1,)), ((), ())),
                preferred_element_type=F32).astype(BF16)


def on_device(tokens, norm_gain, router, down_proj, up_proj, expert_gate, expert_up, expert_down,
              expert_ids, slot_pos, overflow_list):
    rows, width = tokens.shape
    top = expert_ids.shape[1]
    local = expert_gate.shape[0]
    depth, latent = down_proj.shape
    ff = expert_gate.shape[2]
    shards = lax.axis_size("expert")
    copies = lax.axis_size("replica")
    chips = shards // 2
    wide = copies * depth
    spread = copies
    if depth % 128:
        down_proj = lax.all_gather(down_proj, "replica", axis=0, tiled=True)
        up_proj = lax.all_gather(up_proj, "replica", axis=0, tiled=True)
        depth, spread = wide, 1
    experts = shards * local
    e = lax.axis_index("expert")
    r = lax.axis_index("replica")
    pos = jnp.stack([e % 2, e // 2, r if spread > 1 else 0 * r, e]).astype(jnp.int32)

    down = {(0, 0): down_proj}
    for b in range(1, spread):
        down[(0, b)] = swap(down_proj, "replica", b)
    for b in range(spread):
        for a in range(1, chips):
            down[(a, b)] = swap(down[(0, b)], "expert", 2 * a)

    listed = jnp.transpose(overflow_list[0], (1, 0, 2)).reshape(copies, experts)
    keep, send, wt = pl.pallas_call(
        functools.partial(gate_kernel, top, wide),
        out_shape=(
            jax.ShapeDtypeStruct((rows, width // 2), BF16),
            jax.ShapeDtypeStruct((rows, width // 2), BF16),
            jax.ShapeDtypeStruct((experts, rows), F32),
        ),
        in_specs=[SM] + [VM] * 6,
        out_specs=(VM, VM, VM),
        scratch_shapes=[pltpu.VMEM((rows, width), BF16)],
        name="gates", compiler_params=grant(12),
        cost_estimate=cost(4 * rows * width * experts, 3 * rows * width * 2),
    )(pos, tokens, norm_gain.reshape(1, width), router, expert_ids, slot_pos, listed)
    recv = swap(send, "expert", 1)
    wt_core = swap(wt, "expert", 1)

    order = sorted(down)
    partial = pl.pallas_call(
        functools.partial(latent_kernel, order, wide),
        out_shape=jax.ShapeDtypeStruct((2 * rows, latent), F32),
        in_specs=[SM] + [VM] * (2 + len(order)),
        out_specs=VM,
        name="latent", compiler_params=grant(10),
        cost_estimate=cost(2 * rows * width * latent, 4 * width * latent),
    )(pos, keep, recv, *[down[k] for k in order])
    partial_core = swap(partial, "expert", 1)
    lat_own, lat_core = pl.pallas_call(
        finish_kernel,
        out_shape=(jax.ShapeDtypeStruct((rows, latent), BF16),) * 2,
        in_specs=[VM, VM],
        out_specs=(VM, VM),
        name="finish", compiler_params=grant(6),
        cost_estimate=cost(2 * rows * latent, 12 * rows * latent),
    )(partial, partial_core)

    def run(x0, x1, w0, w1):
        return pl.pallas_call(
            functools.partial(expert_kernel, local),
            grid=(local,),
            out_shape=(jax.ShapeDtypeStruct((rows, latent), BF16),) * 2,
            in_specs=[SM] + [VM] * 4 + [
                pl.BlockSpec((1, latent, ff), lambda j: (j, 0, 0)),
                pl.BlockSpec((1, latent, ff), lambda j: (j, 0, 0)),
                pl.BlockSpec((1, ff, latent), lambda j: (j, 0, 0)),
            ],
            out_specs=(VM, VM),
            scratch_shapes=[pltpu.VMEM((2 * rows, latent), F32), pltpu.VMEM((2 * rows, 128), F32)],
            name="experts", compiler_params=grant(24),
            cost_estimate=cost(12 * rows * local * latent * ff, 6 * local * latent * ff),
        )(pos, x0, x1, w0, w1, expert_gate, expert_up, expert_down)

    far = []
    for a in range(1, chips):
        x0 = swap(lat_own, "expert", 2 * a)
        far.append((x0, swap(x0, "expert", 1), swap(wt, "expert", 2 * a), swap(wt_core, "expert", 2 * a)))
    near0, near1 = run(lat_own, lat_core, wt, wt_core)
    sums = [near0, swap(near1, "expert", 1)]
    for a in range(1, chips):
        o0, o1 = run(*far[a - 1])
        back = swap(o1, "expert", 1)
        s = pl.pallas_call(
            add_kernel, out_shape=jax.ShapeDtypeStruct((rows, latent), BF16), in_specs=[VM, VM],
            out_specs=VM, name="add", compiler_params=grant(4), cost_estimate=cost(rows * latent, 6 * rows * latent),
        )(o0, back)
        sums.append(swap(s, "expert", 2 * a))

    pair = jnp.concatenate([up_proj] + [swap(up_proj, "expert", 2 * a) for a in range(1, chips)], axis=0)
    ups = {(0, 0): pair}
    for b in range(1, spread):
        ups[(0, b)] = swap(pair, "replica", b)
    for b in range(spread):
        ups[(1, b)] = swap(ups[(0, b)], "expert", 1)
    order = sorted(ups)
    return pl.pallas_call(
        functools.partial(final_kernel, len(sums), order, spread, depth),
        out_shape=jax.ShapeDtypeStruct((rows, width), BF16),
        in_specs=[SM] + [VM] * (len(sums) + len(order)),
        out_specs=VM,
        name="final", compiler_params=grant(12),
        cost_estimate=cost(2 * rows * width * latent, 4 * width * latent),
    )(pos, *sums, *[ups[k] for k in order])


def solution(mesh):
    placed = (
        P(("groups", "expert", "replica"), None),
        P(),
        P(),
        P(("expert", "replica"), None),
        P(("expert", "replica"), None),
        P("expert", None, None),
        P("expert", None, None),
        P("expert", None, None),
        P(("groups", "expert", "replica"), None),
        P(("groups", "expert", "replica"), None),
        P(("groups", "expert", "replica"), None, None, None),
    )
    return jax.shard_map(
        on_device,
        mesh=mesh,
        in_specs=placed,
        out_specs=P(("groups", "expert", "replica"), None),
        check_vma=False,
    )
```

```python
import functools

import jax
import jax.numpy as jnp
from jax import lax
from jax.experimental import pallas as pl
from jax.experimental.pallas import tpu as pltpu
from jax.sharding import PartitionSpec as P

epsilon = 1e-06
F32 = jnp.float32
BF16 = jnp.bfloat16

VM = pl.BlockSpec(memory_space=pltpu.VMEM)
SM = pl.BlockSpec(memory_space=pltpu.SMEM)
HB = pl.BlockSpec(memory_space=pltpu.HBM)


def swap(x, axis, bits):
    size = lax.axis_size(axis)
    return lax.ppermute(x, axis, [(i, i ^ bits) for i in range(size)])


def swap_pair(x, axes, move):
    sizes = [lax.axis_size(axis) for axis in axes]
    pairs = []
    for i in range(sizes[0]):
        for j in range(sizes[1]):
            p, q = move(i, j)
            pairs.append((i * sizes[1] + j, p * sizes[1] + q))
    return lax.ppermute(x, axes, pairs)


def kernel(body, out_shape, operands, specs, mib, flops=0, nbytes=0, scratch=(), out_specs=None):
    many = isinstance(out_shape, tuple)
    if out_specs is None:
        out_specs = (VM,) * len(out_shape) if many else VM
    return pl.pallas_call(
        body,
        out_shape=out_shape,
        in_specs=specs,
        out_specs=out_specs,
        scratch_shapes=list(scratch),
        compiler_params=pltpu.CompilerParams(vmem_limit_bytes=mib * 1024 * 1024),
        cost_estimate=pl.CostEstimate(flops=flops, bytes_accessed=nbytes, transcendentals=0),
    )(*operands)


def gate_kernel(top, wide, pos_ref, list_ref, tok_ref, gain_ref, router_ref, ids_ref, slot_ref,
                g_ref, u_ref, d_ref, keep_ref, send_ref, wt_ref, g0_ref, u0_ref, d0_ref,
                normed_ref, sem):
    copies = [
        pltpu.make_async_copy(src.at[pl.ds(0, 1)], dst, sem.at[i])
        for i, (src, dst) in enumerate(((g_ref, g0_ref), (u_ref, u0_ref), (d_ref, d0_ref)))
    ]
    for copy in copies:
        copy.start()
    values = tok_ref[...].astype(F32)
    scale = lax.rsqrt(jnp.mean(values * values, axis=-1, keepdims=True) + epsilon)
    normed = (values * scale * gain_ref[...]).astype(BF16)
    normed_ref[...] = normed
    core = pos_ref[0]
    for h in range(keep_ref.shape[1] // wide):
        mine = pl.multiple_of((2 * h + core) * wide, wide)
        other = pl.multiple_of((2 * h + 1 - core) * wide, wide)
        keep_ref[:, h * wide:(h + 1) * wide] = normed_ref[:, pl.ds(mine, wide)]
        send_ref[:, h * wide:(h + 1) * wide] = normed_ref[:, pl.ds(other, wide)]
    logits = lax.dot_general(router_ref[...], normed_ref[...], (((1,), (1,)), ((), ())),
                             preferred_element_type=F32)
    sig = jax.nn.sigmoid(logits)
    experts, rows = sig.shape
    sub = lax.broadcasted_iota(jnp.int32, (experts, rows), 0)
    lane = lax.broadcasted_iota(jnp.int32, (experts, rows), 1)
    total = jnp.zeros((experts, rows), F32)
    served = jnp.zeros((experts, rows), F32)
    for k in range(top):
        hit = sub == ids_ref[k:k + 1, :]
        total = total + jnp.where(hit, 1.0, 0.0)
        served = served + jnp.where(hit & (slot_ref[k:k + 1, :] >= 0), 1.0, 0.0)
    _, shards, copies_n, local = list_ref.shape

    def listed(i, served):
        shard, copy = i // copies_n, i % copies_n
        for m in range(local):
            entry = list_ref[0, shard, copy, m]
            owner = jnp.where(entry >= 0, entry, -top) // top
            served = served + jnp.where((lane == owner) & (sub == shard * local + m), 1.0, 0.0)
        return served

    served = lax.fori_loop(0, shards * copies_n, listed, served)
    denom = jnp.sum(total * sig, axis=0, keepdims=True)
    wt_ref[...] = jnp.where(served > 0.0, sig / denom, 0.0)
    for copy in copies:
        copy.wait()


def latent_kernel(chunks, wide, pos_ref, keep_ref, recv_ref, *refs):
    w_refs, (out_ref, x_ref, w_ref) = refs[:-3], refs[-3:]
    half, rep, group = pos_ref[1], pos_ref[2], pos_ref[4]
    rows = keep_ref.shape[0]
    depth = w_refs[0].shape[0]
    for i, ((a, b), chunk) in enumerate(zip(chunks, w_refs)):
        if b == "A":
            b = 2 + group
        elif b == "B":
            b = 3 - group
        at = pl.multiple_of((half ^ a) * wide + (rep ^ b) * depth, depth)
        x_ref[:rows, i * depth:(i + 1) * depth] = keep_ref[:, pl.ds(at, depth)]
        x_ref[rows:, i * depth:(i + 1) * depth] = recv_ref[:, pl.ds(at, depth)]
        w_ref[i * depth:(i + 1) * depth, :] = chunk[...]
    out_ref[...] = jnp.dot(x_ref[...], w_ref[...], preferred_element_type=F32)


def finish_kernel(mine_ref, recv_ref, own_ref, core_ref):
    rows = own_ref.shape[0]
    own_ref[...] = (mine_ref[:rows, :] + recv_ref[rows:, :]).astype(BF16)
    core_ref[...] = (mine_ref[rows:, :] + recv_ref[:rows, :]).astype(BF16)


def expert(x, weight, gate_w, up_w, down_w):
    gate = jnp.dot(x, gate_w, preferred_element_type=F32)
    upper = jnp.dot(x, up_w, preferred_element_type=F32)
    half = 0.5 * gate
    hidden = ((half + half * jnp.tanh(half)) * upper).astype(BF16)
    result = jnp.dot(hidden, down_w, preferred_element_type=F32).astype(BF16)
    return result.astype(F32) * weight


def columns(me, local, wt_ref):
    _, rows = wt_ref.shape
    wt = wt_ref[...]
    sub = lax.broadcasted_iota(jnp.int32, wt.shape, 0)
    picked = [jnp.sum(jnp.where(sub == me * local + j, wt, 0.0), axis=0, keepdims=True)
              for j in range(local)]
    pad = jnp.zeros((-local % 8, rows), F32)
    return jnp.concatenate(picked + [pad], axis=0).T


def near_kernel(local, pos_ref, x0_ref, x1_ref, w0_ref, w1_ref, g0_ref, u0_ref, d0_ref,
                g_ref, u_ref, d_ref, o0_ref, o1_ref, gv_ref, uv_ref, dv_ref, acc_ref, sem):
    copies = {}
    for j in range(1, local):
        for i, (src, dst) in enumerate(((g_ref, gv_ref), (u_ref, uv_ref), (d_ref, dv_ref))):
            copies[j, i] = pltpu.make_async_copy(src.at[pl.ds(j, 1)], dst.at[pl.ds(j - 1, 1)],
                                                 sem.at[i, j - 1])
            copies[j, i].start()
    rows = x0_ref.shape[0]
    cols = [columns(pos_ref[3], local, w) for w in (w0_ref, w1_ref)]
    for j in range(local):
        if j == 0:
            weights = g0_ref[0], u0_ref[0], d0_ref[0]
        else:
            for i in range(3):
                copies[j, i].wait()
            weights = gv_ref[j - 1], uv_ref[j - 1], dv_ref[j - 1]
        for i, x_ref in enumerate((x0_ref, x1_ref)):
            part = expert(x_ref[...], cols[i][:, j:j + 1], *weights)
            span = slice(i * rows, (i + 1) * rows)
            acc_ref[span, :] = part if j == 0 else acc_ref[span, :] + part
    o0_ref[...] = acc_ref[:rows, :].astype(BF16)
    o1_ref[...] = acc_ref[rows:, :].astype(BF16)


def far_kernel(local, pos_ref, x_ref, w_ref, g0_ref, u0_ref, d0_ref, gv_ref, uv_ref, dv_ref,
               o_ref, acc_ref):
    cols = columns(pos_ref[3], local, w_ref)
    for j in range(local):
        if j == 0:
            weights = g0_ref[0], u0_ref[0], d0_ref[0]
        else:
            weights = gv_ref[j - 1], uv_ref[j - 1], dv_ref[j - 1]
        part = expert(x_ref[...], cols[:, j:j + 1], *weights)
        acc_ref[...] = part if j == 0 else acc_ref[...] + part
    o_ref[...] = acc_ref[...].astype(BF16)


def add_kernel(a_ref, b_ref, o_ref):
    o_ref[...] = (a_ref[...].astype(F32) + b_ref[...].astype(F32)).astype(BF16)


def join_kernel(*refs):
    depth = refs[0].shape[0]
    for i, x_ref in enumerate(refs[:-1]):
        refs[-1][i * depth:(i + 1) * depth, :] = x_ref[...]


def final_kernel(n_sum, chunks, copies, depth, pos_ref, *refs):
    out_ref = refs[-1]
    half, rep, core = pos_ref[1], pos_ref[2], pos_ref[0]
    total = refs[0][...].astype(F32)
    for s_ref in refs[1:n_sum]:
        total = total + s_ref[...].astype(F32)
    merged = total.astype(BF16)
    for (c, b), w_ref in zip(chunks, refs[n_sum:-1]):
        block = lax.dot_general(merged, w_ref[...], (((1,), (1,)), ((), ())),
                                preferred_element_type=F32).astype(BF16)
        for a in range(w_ref.shape[0] // depth):
            e = 2 * (half ^ a) + (core ^ c)
            at = pl.multiple_of((e * copies + (rep ^ b)) * depth, depth)
            out_ref[:, pl.ds(at, depth)] = block[:, a * depth:(a + 1) * depth]


def shape(dims, dtype=BF16):
    return jax.ShapeDtypeStruct(dims, dtype)


def on_device(tokens, norm_gain, router, down_proj, up_proj, expert_gate, expert_up, expert_down,
              expert_ids, slot_pos, overflow_list):
    rows, width = tokens.shape
    top = expert_ids.shape[1]
    local, _, ff = expert_gate.shape
    depth, latent = down_proj.shape
    groups = lax.axis_size("groups")
    shards = lax.axis_size("expert")
    copies = lax.axis_size("replica")
    chips = shards // 2
    wide = copies * depth
    spread = copies
    if depth % 128:
        down_proj = lax.all_gather(down_proj, "replica", axis=0, tiled=True)
        up_proj = lax.all_gather(up_proj, "replica", axis=0, tiled=True)
        depth, spread = wide, 1
    experts = shards * local
    g = lax.axis_index("groups")
    e = lax.axis_index("expert")
    r = lax.axis_index("replica")
    pos = jnp.stack([e % 2, e // 2, r if spread > 1 else 0 * r, e, g]).astype(jnp.int32)

    down = {(0, 0): down_proj}
    if spread == groups + 2 and groups == 2:
        near_z = swap(down_proj, "replica", 1)
        far_z = swap_pair(down_proj, ("groups", "replica"), lambda i, j: (i, j ^ (2 + i)))
        down[(0, 1)] = near_z
        down[(0, "A")] = far_z
        for a in range(1, chips):
            down[(a, 0)] = swap(down_proj, "expert", 2 * a)
        ups_x = [swap(up_proj, "expert", 2 * a) for a in range(1, chips)]
        for a in range(1, chips):
            down[(a, 1)] = swap(near_z, "expert", 2 * a)
            down[(a, "B")] = swap_pair(far_z, ("groups", "expert"),
                                       lambda i, j: (i ^ 1, j ^ (2 * a)))
            down[(a, "A")] = swap(far_z, "expert", 2 * a)
        down[(0, "B")] = swap(far_z, "groups", 1)
    else:
        for b in range(1, spread):
            down[(0, b)] = swap(down_proj, "replica", b)
        for b in range(spread):
            for a in range(1, chips):
                down[(a, b)] = swap(down[(0, b)], "expert", 2 * a)
        ups_x = [swap(up_proj, "expert", 2 * a) for a in range(1, chips)]

    one = [shape((1,) + w.shape[1:]) for w in (expert_gate, expert_up, expert_down)]
    rest = [shape((local - 1,) + w.shape[1:]) for w in (expert_gate, expert_up, expert_down)]
    keep, send, wt, *first = kernel(
        functools.partial(gate_kernel, top, wide),
        (shape((rows, width // 2)), shape((rows, width // 2)), shape((experts, rows), F32), *one),
        (pos, overflow_list, tokens, norm_gain.reshape(1, width), router.T, expert_ids.T,
         slot_pos.T, expert_gate, expert_up, expert_down),
        [SM, SM] + [VM] * 5 + [HB] * 3, 20, 4 * rows * width * experts, 4 * rows * width,
        [pltpu.VMEM((rows, width), BF16), pltpu.SemaphoreType.DMA((3,))])
    recv = swap(send, "expert", 1)
    wt_core = swap(wt, "expert", 1)

    order = list(down)
    partial = kernel(
        functools.partial(latent_kernel, order, wide), shape((2 * rows, latent), F32),
        (pos, keep, recv, *[down[k] for k in order]), [SM] + [VM] * (2 + len(order)), 14,
        2 * rows * width * latent, 2 * width * latent,
        [pltpu.VMEM((2 * rows, width // 2), BF16), pltpu.VMEM((width // 2, latent), BF16)])
    partial_core = swap(partial, "expert", 1)
    lat_own, lat_core = kernel(
        finish_kernel, (shape((rows, latent)),) * 2, (partial, partial_core), [VM, VM], 6,
        2 * rows * latent, 12 * rows * latent)

    far = []
    for a in range(1, chips):
        x0 = swap(lat_own, "expert", 2 * a)
        w0 = swap(wt, "expert", 2 * a)
        far.append((x0, w0, swap(x0, "expert", 1), swap(w0, "expert", 1)))
    work = 6 * rows * local * latent * ff
    near0, near1, *kept = kernel(
        functools.partial(near_kernel, local),
        (shape((rows, latent)), shape((rows, latent)), *rest),
        (pos, lat_own, lat_core, wt, wt_core, *first, expert_gate, expert_up, expert_down),
        [SM] + [VM] * 7 + [HB] * 3, 28, 2 * work, 6 * local * latent * ff,
        [pltpu.VMEM((2 * rows, latent), F32), pltpu.SemaphoreType.DMA((3, local - 1))])

    def run_far(x, w):
        return kernel(functools.partial(far_kernel, local), shape((rows, latent)),
                      (pos, x, w, *first, *kept), [SM] + [VM] * 8, 20, work, 6 * local * latent * ff,
                      [pltpu.VMEM((rows, latent), F32)])

    sums = [near0, swap(near1, "expert", 1)]
    for a in range(1, chips):
        x0, w0, x1, w1 = far[a - 1]
        o0 = run_far(x0, w0)
        o1 = run_far(x1, w1)
        back = swap(o1, "expert", 1)
        s = kernel(add_kernel, shape((rows, latent)), (o0, back), [VM, VM], 4,
                   rows * latent, 6 * rows * latent)
        sums.append(swap(s, "expert", 2 * a))

    pair = kernel(join_kernel, shape((chips * depth, latent)), (up_proj, *ups_x),
                  [VM] * chips, 4, 0, 4 * chips * depth * latent)
    ups = {(0, 0): pair}
    for b in range(1, spread):
        ups[(0, b)] = swap(pair, "replica", b)
    for b in range(spread):
        ups[(1, b)] = swap(ups[(0, b)], "expert", 1)
    order = sorted(ups)
    return kernel(
        functools.partial(final_kernel, len(sums), order, spread, depth),
        shape((rows, width)), (pos, *sums, *[ups[k] for k in order]),
        [SM] + [VM] * (len(sums) + len(order)), 14, 2 * rows * width * latent, 2 * width * latent)


def solution(mesh):
    placed = (
        P(("groups", "expert", "replica"), None),
        P(),
        P(),
        P(("expert", "replica"), None),
        P(("expert", "replica"), None),
        P("expert", None, None),
        P("expert", None, None),
        P("expert", None, None),
        P(("groups", "expert", "replica"), None),
        P(("groups", "expert", "replica"), None),
        P(("groups", "expert", "replica"), None, None, None),
    )

    return jax.shard_map(
        on_device,
        mesh=mesh,
        in_specs=placed,
        out_specs=P(("groups", "expert", "replica"), None),
        check_vma=False,
    )
```

```python
import functools

import jax
import jax.numpy as jnp
from jax import lax
from jax.experimental import pallas as pl
from jax.experimental.pallas import tpu as pltpu
from jax.sharding import PartitionSpec as P

epsilon = 1e-06
F32 = jnp.float32
BF16 = jnp.bfloat16

VM = pl.BlockSpec(memory_space=pltpu.VMEM)
SM = pl.BlockSpec(memory_space=pltpu.SMEM)
AN = pl.BlockSpec(memory_space=pl.ANY)


def in_hbm(x):
    return pltpu.with_memory_space_constraint(x, pltpu.HBM)


def swap(x, axis, bits):
    size = lax.axis_size(axis)
    return lax.ppermute(x, axis, [(i, i ^ bits) for i in range(size)])


def swap_pair(x, axes, move):
    sizes = [lax.axis_size(axis) for axis in axes]
    pairs = []
    for i in range(sizes[0]):
        for j in range(sizes[1]):
            p, q = move(i, j)
            pairs.append((i * sizes[1] + j, p * sizes[1] + q))
    return lax.ppermute(x, axes, pairs)


def kernel(body, out_shape, operands, specs, mib, flops=0, nbytes=0, scratch=(), out_specs=None):
    many = isinstance(out_shape, tuple)
    if out_specs is None:
        out_specs = (VM,) * len(out_shape) if many else VM
    return pl.pallas_call(
        body,
        out_shape=out_shape,
        in_specs=specs,
        out_specs=out_specs,
        scratch_shapes=list(scratch),
        compiler_params=pltpu.CompilerParams(vmem_limit_bytes=mib * 1024 * 1024),
        cost_estimate=pl.CostEstimate(flops=flops, bytes_accessed=nbytes, transcendentals=0),
    )(*operands)


def gate_kernel(top, wide, pos_ref, list_ref, tok_hbm, gain_hbm, router_hbm, ids_hbm, slot_hbm,
                keep_ref, send_ref, wt_ref, normed_ref, tok_ref, gain_ref, router_ref, ids_ref,
                slot_ref, sem):
    pairs = ((tok_hbm, tok_ref), (gain_hbm, gain_ref), (router_hbm, router_ref),
             (ids_hbm, ids_ref), (slot_hbm, slot_ref))
    copies = [pltpu.make_async_copy(src, dst, sem.at[i]) for i, (src, dst) in enumerate(pairs)]
    for copy in copies:
        copy.start()
    for copy in copies:
        copy.wait()
    values = tok_ref[...].astype(F32)
    scale = lax.rsqrt(jnp.mean(values * values, axis=-1, keepdims=True) + epsilon)
    normed = (values * scale * gain_ref[...]).astype(BF16)
    normed_ref[...] = normed
    core = pos_ref[0]
    for h in range(keep_ref.shape[1] // wide):
        mine = pl.multiple_of((2 * h + core) * wide, wide)
        other = pl.multiple_of((2 * h + 1 - core) * wide, wide)
        keep_ref[:, h * wide:(h + 1) * wide] = normed_ref[:, pl.ds(mine, wide)]
        send_ref[:, h * wide:(h + 1) * wide] = normed_ref[:, pl.ds(other, wide)]
    logits = lax.dot_general(router_ref[...], normed_ref[...], (((1,), (1,)), ((), ())),
                             preferred_element_type=F32)
    sig = jax.nn.sigmoid(logits)
    experts, rows = sig.shape
    sub = lax.broadcasted_iota(jnp.int32, (experts, rows), 0)
    lane = lax.broadcasted_iota(jnp.int32, (experts, rows), 1)
    total = jnp.zeros((experts, rows), F32)
    served = jnp.zeros((experts, rows), F32)
    for k in range(top):
        hit = sub == ids_ref[k:k + 1, :]
        total = total + jnp.where(hit, 1.0, 0.0)
        served = served + jnp.where(hit & (slot_ref[k:k + 1, :] >= 0), 1.0, 0.0)
    _, shards, copies_n, local = list_ref.shape

    def listed(i, served):
        shard, copy = i // copies_n, i % copies_n
        for m in range(local):
            entry = list_ref[0, shard, copy, m]
            owner = jnp.where(entry >= 0, entry, -top) // top
            served = served + jnp.where((lane == owner) & (sub == shard * local + m), 1.0, 0.0)
        return served

    served = lax.fori_loop(0, shards * copies_n, listed, served)
    denom = jnp.sum(total * sig, axis=0, keepdims=True)
    wt_ref[...] = jnp.where(served > 0.0, sig / denom, 0.0)


def latent_kernel(chunks, wide, pos_ref, keep_ref, recv_ref, wt_ref, *refs):
    w_refs, (out_ref, x_ref, w_ref, sem) = refs[:-4], refs[-4:]
    half, rep, group = pos_ref[1], pos_ref[2], pos_ref[4]
    rows = keep_ref.shape[0]
    depth = w_refs[0].shape[0]
    load = pltpu.make_async_copy(w_refs[0], w_ref.at[pl.ds(0, depth)], sem)
    load.start()
    for i, ((a, b), chunk) in enumerate(zip(chunks, w_refs)):
        if b == "A":
            b = 2 + group
        elif b == "B":
            b = 3 - group
        at = pl.multiple_of((half ^ a) * wide + (rep ^ b) * depth, depth)
        x_ref[:rows, i * depth:(i + 1) * depth] = keep_ref[:, pl.ds(at, depth)]
        x_ref[rows:, i * depth:(i + 1) * depth] = recv_ref[:, pl.ds(at, depth)]
        if i:
            w_ref[i * depth:(i + 1) * depth, :] = chunk[...]
    load.wait()
    out_ref[:2 * rows, :] = jnp.dot(x_ref[...], w_ref[...], preferred_element_type=F32)
    out_ref[2 * rows:, :rows] = wt_ref[...]
    out_ref[2 * rows:, rows:] = jnp.zeros_like(out_ref[2 * rows:, rows:])


def finish_kernel(mine_ref, recv_ref, own_ref, core_ref):
    rows = (own_ref.shape[1]) // 2
    own_ref[:rows, :] = (mine_ref[:rows, :] + recv_ref[rows:2 * rows, :]).astype(BF16)
    core_ref[:rows, :] = (mine_ref[rows:2 * rows, :] + recv_ref[:rows, :]).astype(BF16)
    for src, dst in ((mine_ref, own_ref), (recv_ref, core_ref)):
        wt = src[2 * rows:, :rows]
        lead = wt.astype(BF16)
        dst[rows:, :rows] = lead
        dst[rows:, rows:] = (wt - lead.astype(F32)).astype(BF16)


def expert(x, weight, gate_w, up_w, down_w):
    gate = jnp.dot(x, gate_w, preferred_element_type=F32)
    upper = jnp.dot(x, up_w, preferred_element_type=F32)
    half = 0.5 * gate
    hidden = ((half + half * jnp.tanh(half)) * upper).astype(BF16)
    result = jnp.dot(hidden, down_w, preferred_element_type=F32).astype(BF16)
    return result.astype(F32) * weight


def columns(me, local, pay_ref, at, size):
    rows = pay_ref.shape[1] // 2
    wt = (pay_ref[rows:, at:at + size].astype(F32)
          + pay_ref[rows:, rows + at:rows + at + size].astype(F32))
    sub = lax.broadcasted_iota(jnp.int32, wt.shape, 0)
    picked = [jnp.sum(jnp.where(sub == me * local + j, wt, 0.0), axis=0, keepdims=True)
              for j in range(local)]
    pad = jnp.zeros((-local % 8, size), F32)
    return jnp.concatenate(picked + [pad], axis=0).T


def near_kernel(local, held, pos_ref, x0_ref, x1_ref, g_ref, u_ref, d_hbm, o0_ref, o1_ref, d_ref,
                acc_ref, sem):
    loads = [pltpu.make_async_copy(d_hbm.at[pl.ds(j, 1)], d_ref.at[pl.ds(j, 1)], sem.at[j])
             for j in range(local)]
    for load in loads:
        load.start()
    rows = o0_ref.shape[0]
    cols = [columns(pos_ref[3], local, p, 0, rows) for p in (x0_ref, x1_ref)]
    for j in range(local):
        loads[j].wait()
        weights = g_ref[j], u_ref[j], d_ref[j]
        part = expert(x1_ref[:rows, :], cols[1][:, j:j + 1], *weights)
        acc_ref[...] = part if j == 0 else acc_ref[...] + part
        if j < local - held:
            part = expert(x0_ref[:rows, :], cols[0][:, j:j + 1], *weights)
            o0_ref[...] = part if j == 0 else o0_ref[...] + part
    o1_ref[...] = acc_ref[...].astype(BF16)


def rest_kernel(local, held, pos_ref, x_ref, a_ref, g_ref, u_ref, d_ref, o_ref):
    rows = o_ref.shape[0]
    cols = columns(pos_ref[3], local, x_ref, 0, rows)
    o_ref[...] = a_ref[...]
    for j in range(local - held, local):
        o_ref[...] += expert(x_ref[:rows, :], cols[:, j:j + 1], g_ref[j], u_ref[j], d_ref[j])


def far_kernel(local, at, pos_ref, x0_ref, x1_ref, g_ref, u_ref, d_ref, o0_ref, o1_ref, x_ref, acc_ref):
    size = o0_ref.shape[0]
    x_ref[:size, :] = x0_ref[at:at + size, :]
    x_ref[size:, :] = x1_ref[at:at + size, :]
    cols = jnp.concatenate([columns(pos_ref[3], local, p, at, size) for p in (x0_ref, x1_ref)], axis=0)
    for j in range(local):
        part = expert(x_ref[...], cols[:, j:j + 1], g_ref[j], u_ref[j], d_ref[j])
        acc_ref[...] = part if j == 0 else acc_ref[...] + part
    o0_ref[...] = acc_ref[:size, :].astype(BF16)
    o1_ref[...] = acc_ref[size:, :].astype(BF16)


def add_kernel(a_ref, b_ref, o_ref):
    o_ref[...] = (a_ref[...].astype(F32) + b_ref[...].astype(F32)).astype(BF16)


def join_kernel(own_ref, *refs):
    x_refs, (out_ref, held_ref, sem) = refs[:-3], refs[-3:]
    depth = own_ref.shape[0]
    load = pltpu.make_async_copy(own_ref, held_ref, sem)
    load.start()
    for i, x_ref in enumerate(x_refs):
        out_ref[:, (i + 1) * depth:(i + 2) * depth] = x_ref[...].T
    load.wait()
    out_ref[:, :depth] = held_ref[...].T


def final_kernel(n_sum, parts, chunks, copies, depth, pos_ref, *refs):
    out_ref, block_ref, sem = refs[-3:]
    half, rep, core = pos_ref[1], pos_ref[2], pos_ref[0]
    total = refs[0][...].astype(F32)
    for s_ref in refs[1:n_sum]:
        total = total + s_ref[...].astype(F32)
    back = refs[n_sum:n_sum + parts]
    total = total + jnp.concatenate([s_ref[...].astype(F32) for s_ref in back], axis=0)
    merged = total.astype(BF16)
    outs = []
    for i, ((c, b), w_ref) in enumerate(zip(chunks, refs[n_sum + parts:-3])):
        block_ref[i] = jnp.dot(merged, w_ref[...], preferred_element_type=F32).astype(BF16)
        for a in range(w_ref.shape[1] // depth):
            e = 2 * (half ^ a) + (core ^ c)
            at = pl.multiple_of((e * copies + (rep ^ b)) * depth, depth)
            outs.append(pltpu.make_async_copy(block_ref.at[i, :, pl.ds(a * depth, depth)],
                                              out_ref.at[:, pl.ds(at, depth)], sem.at[i, a]))
            outs[-1].start()
    for out in outs:
        out.wait()


def shape(dims, dtype=BF16):
    return jax.ShapeDtypeStruct(dims, dtype)


def on_device(tokens, norm_gain, router, down_proj, up_proj, expert_gate, expert_up, expert_down,
              expert_ids, slot_pos, overflow_list):
    rows, width = tokens.shape
    top = expert_ids.shape[1]
    local, _, ff = expert_gate.shape
    depth, latent = down_proj.shape
    groups = lax.axis_size("groups")
    shards = lax.axis_size("expert")
    copies = lax.axis_size("replica")
    chips = shards // 2
    wide = copies * depth
    spread = copies
    if depth % 128:
        down_proj = lax.all_gather(down_proj, "replica", axis=0, tiled=True)
        up_proj = lax.all_gather(up_proj, "replica", axis=0, tiled=True)
        depth, spread = wide, 1
    experts = shards * local
    g = lax.axis_index("groups")
    e = lax.axis_index("expert")
    r = lax.axis_index("replica")
    pos = jnp.stack([e % 2, e // 2, r if spread > 1 else 0 * r, e, g]).astype(jnp.int32)

    down = {(0, 0): down_proj}
    if spread == groups + 2 and groups == 2:
        near_z = swap(down_proj, "replica", 1)
        far_z = swap_pair(down_proj, ("groups", "replica"), lambda i, j: (i, j ^ (2 + i)))
        down[(0, 1)] = near_z
        down[(0, "A")] = far_z
        for a in range(1, chips):
            down[(a, 0)] = swap(down_proj, "expert", 2 * a)
        ups_x = [swap(up_proj, "expert", 2 * a) for a in range(1, chips)]
        for a in range(1, chips):
            down[(a, 1)] = swap(near_z, "expert", 2 * a)
            down[(a, "B")] = swap_pair(far_z, ("groups", "expert"),
                                       lambda i, j: (i ^ 1, j ^ (2 * a)))
            down[(a, "A")] = swap(far_z, "expert", 2 * a)
        down[(0, "B")] = swap(far_z, "groups", 1)
    else:
        for b in range(1, spread):
            down[(0, b)] = swap(down_proj, "replica", b)
        for b in range(spread):
            for a in range(1, chips):
                down[(a, b)] = swap(down[(0, b)], "expert", 2 * a)
        ups_x = [swap(up_proj, "expert", 2 * a) for a in range(1, chips)]

    keep, send, wt = kernel(
        functools.partial(gate_kernel, top, wide),
        (shape((rows, width // 2)), shape((rows, width // 2)), shape((experts, rows), F32)),
        (pos, overflow_list, *map(in_hbm, (
            tokens, norm_gain.reshape(1, width), router.T, expert_ids.T, slot_pos.T))),
        [SM, SM] + [AN] * 5, 20, 4 * rows * width * experts, 4 * rows * width,
        [pltpu.VMEM((rows, width), BF16), pltpu.VMEM((rows, width), BF16), pltpu.VMEM((1, width), F32),
         pltpu.VMEM((experts, width), BF16), pltpu.VMEM((top, rows), jnp.int32),
         pltpu.VMEM((top, rows), jnp.int32), pltpu.SemaphoreType.DMA((5,))])
    recv = swap(send, "expert", 1)

    order = list(down)
    partial = kernel(
        functools.partial(latent_kernel, order, wide), shape((2 * rows + experts, latent), F32),
        (pos, keep, recv, wt, in_hbm(down_proj), *[down[k] for k in order[1:]]),
        [SM] + [VM] * 3 + [AN] + [VM] * (len(order) - 1), 14, 2 * rows * width * latent, 2 * width * latent,
        [pltpu.VMEM((2 * rows, width // 2), BF16), pltpu.VMEM((width // 2, latent), BF16),
         pltpu.SemaphoreType.DMA])
    partial_core = swap(partial, "expert", 1)
    own, core = kernel(
        finish_kernel, (shape((rows + experts, latent)),) * 2, (partial, partial_core), [VM, VM],
        6, 2 * rows * latent, 12 * rows * latent)

    work = 6 * rows * latent * ff
    load = 6 * latent * ff
    held = 1
    far = []
    for a in range(1, chips):
        x0 = swap(own, "expert", 2 * a)
        far.append((x0, swap(x0, "expert", 1)))
    near0, near1, kept = kernel(
        functools.partial(near_kernel, local, held),
        (shape((rows, latent), F32), shape((rows, latent)), shape(expert_down.shape)),
        (pos, own, core, expert_gate, expert_up, in_hbm(expert_down)), [SM] + [VM] * 4 + [AN], 20,
        (2 * local - held) * work, local * load,
        [pltpu.VMEM((rows, latent), F32), pltpu.SemaphoreType.DMA((local,))])
    weights = (expert_gate, expert_up, kept)
    near0 = kernel(
        functools.partial(rest_kernel, local, held), shape((rows, latent), F32),
        (pos, own, near0, *weights), [SM] + [VM] * 5, 20, held * work, held * load)
    sums = [near0, swap(near1, "expert", 1)]
    parts = 2
    size = rows // parts
    back = []
    for a in range(1, chips):
        back.append([])
        for h in range(parts):
            o0, o1 = kernel(
                functools.partial(far_kernel, local, h * size), (shape((size, latent)),) * 2,
                (pos, *far[a - 1], *weights), [SM] + [VM] * 5, 20, local * work, local * load,
                [pltpu.VMEM((2 * size, latent), BF16), pltpu.VMEM((2 * size, latent), F32)])
            other = swap(o1, "expert", 1)
            s = kernel(add_kernel, shape((size, latent)), (o0, other), [VM, VM], 4,
                       size * latent, 6 * size * latent)
            back[-1].append(swap(s, "expert", 2 * a))
    for more in back[1:]:
        sums.append(jnp.concatenate(more, axis=0))

    pair = kernel(join_kernel, shape((latent, chips * depth)), (in_hbm(up_proj), *ups_x),
                  [AN] + [VM] * (chips - 1), 4, 0, 4 * chips * depth * latent,
                  [pltpu.VMEM((depth, latent), BF16), pltpu.SemaphoreType.DMA])
    ups = {(0, 0): pair}
    for b in range(1, spread):
        ups[(0, b)] = swap(pair, "replica", b)
    for b in range(spread):
        ups[(1, b)] = swap(ups[(0, b)], "expert", 1)
    order = sorted(ups)
    return kernel(
        functools.partial(final_kernel, len(sums), parts, order, spread, depth),
        shape((rows, width)), (pos, *sums, *back[0], *[ups[k] for k in order]),
        [SM] + [VM] * (len(sums) + parts + len(order)), 14, 2 * rows * width * latent, 2 * width * latent,
        [pltpu.VMEM((len(order), rows, chips * depth), BF16), pltpu.SemaphoreType.DMA((len(order), chips))],
        AN)


def solution(mesh):
    placed = (
        P(("groups", "expert", "replica"), None),
        P(),
        P(),
        P(("expert", "replica"), None),
        P(("expert", "replica"), None),
        P("expert", None, None),
        P("expert", None, None),
        P("expert", None, None),
        P(("groups", "expert", "replica"), None),
        P(("groups", "expert", "replica"), None),
        P(("groups", "expert", "replica"), None, None, None),
    )

    return jax.shard_map(
        on_device,
        mesh=mesh,
        in_specs=placed,
        out_specs=P(("groups", "expert", "replica"), None),
        check_vma=False,
    )
```

```python
import functools

import jax
import jax.numpy as jnp
from jax import lax
from jax.experimental import pallas as pl
from jax.experimental.pallas import tpu as pltpu
from jax.sharding import PartitionSpec as P

epsilon = 1e-06
F32 = jnp.float32
BF16 = jnp.bfloat16

VM = pl.BlockSpec(memory_space=pltpu.VMEM)
SM = pl.BlockSpec(memory_space=pltpu.SMEM)
AN = pl.BlockSpec(memory_space=pl.ANY)


def in_hbm(x):
    return pltpu.with_memory_space_constraint(x, pltpu.HBM)


def swap(x, axis, bits):
    size = lax.axis_size(axis)
    return lax.ppermute(x, axis, [(i, i ^ bits) for i in range(size)])


def swap_pair(x, axes, move):
    sizes = [lax.axis_size(axis) for axis in axes]
    pairs = []
    for i in range(sizes[0]):
        for j in range(sizes[1]):
            p, q = move(i, j)
            pairs.append((i * sizes[1] + j, p * sizes[1] + q))
    return lax.ppermute(x, axes, pairs)


def kernel(body, out_shape, operands, specs, mib, flops=0, nbytes=0, scratch=(), out_specs=None,
           aliases={}):
    many = isinstance(out_shape, tuple)
    if out_specs is None:
        out_specs = (VM,) * len(out_shape) if many else VM
    return pl.pallas_call(
        body,
        out_shape=out_shape,
        in_specs=specs,
        out_specs=out_specs,
        scratch_shapes=list(scratch),
        input_output_aliases=aliases,
        compiler_params=pltpu.CompilerParams(vmem_limit_bytes=mib * 1024 * 1024),
        cost_estimate=pl.CostEstimate(flops=flops, bytes_accessed=nbytes, transcendentals=0),
    )(*operands)


def norm_kernel(wide, pos_ref, tok_hbm, gain_hbm, keep_ref, send_ref, normed_ref, tok_ref, gain_ref, sem):
    pairs = ((tok_hbm, tok_ref), (gain_hbm, gain_ref))
    copies = [pltpu.make_async_copy(src, dst, sem.at[i]) for i, (src, dst) in enumerate(pairs)]
    for copy in copies:
        copy.start()
    for copy in copies:
        copy.wait()
    values = tok_ref[...].astype(F32)
    scale = lax.rsqrt(jnp.mean(values * values, axis=-1, keepdims=True) + epsilon)
    normed_ref[...] = (values * scale * gain_ref[...]).astype(BF16)
    core = pos_ref[0]
    for h in range(keep_ref.shape[1] // wide):
        mine = pl.multiple_of((2 * h + core) * wide, wide)
        other = pl.multiple_of((2 * h + 1 - core) * wide, wide)
        keep_ref[:, h * wide:(h + 1) * wide] = normed_ref[:, pl.ds(mine, wide)]
        send_ref[:, h * wide:(h + 1) * wide] = normed_ref[:, pl.ds(other, wide)]


def gate_kernel(top, normed_ref, list_hbm, router_hbm, ids_hbm, slot_hbm, down_hbm, up_hbm, last_hbm,
                wt_ref, down_ref, up_ref, last_ref, list_ref, router_ref, ids_ref, slot_ref, sem):
    pairs = ((router_hbm, router_ref), (ids_hbm, ids_ref), (slot_hbm, slot_ref), (list_hbm, list_ref),
             (up_hbm, up_ref), (down_hbm, down_ref), (last_hbm, last_ref))
    copies = [pltpu.make_async_copy(src, dst, sem.at[i]) for i, (src, dst) in enumerate(pairs)]
    for copy in copies:
        copy.start()
    for copy in copies[:4]:
        copy.wait()
    logits = lax.dot_general(router_ref[...], normed_ref[...], (((1,), (1,)), ((), ())),
                             preferred_element_type=F32)
    sig = jax.nn.sigmoid(logits)
    experts, rows = sig.shape
    sub = lax.broadcasted_iota(jnp.int32, (experts, rows), 0)
    lane = lax.broadcasted_iota(jnp.int32, (experts, rows), 1)
    total = jnp.zeros((experts, rows), F32)
    served = jnp.zeros((experts, rows), F32)
    for k in range(top):
        hit = sub == ids_ref[k:k + 1, :]
        total = total + jnp.where(hit, 1.0, 0.0)
        served = served + jnp.where(hit & (slot_ref[k:k + 1, :] >= 0), 1.0, 0.0)
    _, shards, copies_n, local = list_ref.shape

    def listed(i, served):
        shard, copy = i // copies_n, i % copies_n
        for m in range(local):
            entry = list_ref[0, shard, copy, m]
            owner = jnp.where(entry >= 0, entry, -top) // top
            served = served + jnp.where((lane == owner) & (sub == shard * local + m), 1.0, 0.0)
        return served

    served = lax.fori_loop(0, shards * copies_n, listed, served)
    denom = jnp.sum(total * sig, axis=0, keepdims=True)
    wt_ref[...] = jnp.where(served > 0.0, sig / denom, 0.0)
    for copy in copies[4:]:
        copy.wait()


def partial_sum(chunks, wide, pos_ref, keep_ref, recv_ref, w_refs, x_ref, w_ref):
    half, rep, group = pos_ref[1], pos_ref[2], pos_ref[4]
    rows = keep_ref.shape[0]
    depth = w_refs[0].shape[0]
    for i, ((a, b), chunk) in enumerate(zip(chunks, w_refs)):
        if b == "A":
            b = 2 + group
        elif b == "B":
            b = 3 - group
        at = pl.multiple_of((half ^ a) * wide + (rep ^ b) * depth, depth)
        x_ref[:rows, i * depth:(i + 1) * depth] = keep_ref[:, pl.ds(at, depth)]
        x_ref[rows:, i * depth:(i + 1) * depth] = recv_ref[:, pl.ds(at, depth)]
        w_ref[i * depth:(i + 1) * depth, :] = chunk[...]
    return jnp.dot(x_ref[...], w_ref[...], preferred_element_type=F32)


def early_kernel(chunks, wide, pos_ref, keep_ref, recv_ref, *refs):
    w_refs, (out_ref, x_ref, w_ref) = refs[:-3], refs[-3:]
    out_ref[...] = partial_sum(chunks, wide, pos_ref, keep_ref, recv_ref, w_refs, x_ref, w_ref)


def late_kernel(chunks, wide, pos_ref, keep_ref, recv_ref, sum_ref, wt_ref, *refs):
    w_refs, (out_ref, x_ref, w_ref) = refs[:-3], refs[-3:]
    rows = keep_ref.shape[0]
    out_ref[2 * rows:, :rows] = wt_ref[...]
    out_ref[2 * rows:, rows:] = jnp.zeros_like(out_ref[2 * rows:, rows:])
    out_ref[:2 * rows, :] = sum_ref[...] + partial_sum(
        chunks, wide, pos_ref, keep_ref, recv_ref, w_refs, x_ref, w_ref)


def finish_kernel(mine_ref, recv_ref, own_ref, core_ref):
    rows = (own_ref.shape[1]) // 2
    own_ref[:rows, :] = (mine_ref[:rows, :] + recv_ref[rows:2 * rows, :]).astype(BF16)
    core_ref[:rows, :] = (mine_ref[rows:2 * rows, :] + recv_ref[:rows, :]).astype(BF16)
    for src, dst in ((mine_ref, own_ref), (recv_ref, core_ref)):
        wt = src[2 * rows:, :rows]
        lead = wt.astype(BF16)
        dst[rows:, :rows] = lead
        dst[rows:, rows:] = (wt - lead.astype(F32)).astype(BF16)


def expert(x, weight, gate_w, up_w, down_w):
    gate = jnp.dot(x, gate_w, preferred_element_type=F32)
    upper = jnp.dot(x, up_w, preferred_element_type=F32)
    half = 0.5 * gate
    hidden = ((half + half * jnp.tanh(half)) * upper).astype(BF16)
    result = jnp.dot(hidden, down_w, preferred_element_type=F32).astype(BF16)
    return result.astype(F32) * weight


def columns(me, local, pay_ref, at, size):
    rows = pay_ref.shape[1] // 2
    wt = (pay_ref[rows:, at:at + size].astype(F32)
          + pay_ref[rows:, rows + at:rows + at + size].astype(F32))
    sub = lax.broadcasted_iota(jnp.int32, wt.shape, 0)
    picked = [jnp.sum(jnp.where(sub == me * local + j, wt, 0.0), axis=0, keepdims=True)
              for j in range(local)]
    pad = jnp.zeros((-local % 8, size), F32)
    return jnp.concatenate(picked + [pad], axis=0).T


def near_kernel(local, pos_ref, x0_ref, x1_ref, g_ref, u_ref, d_ref, o0_ref, o1_ref, acc_ref):
    rows = o0_ref.shape[0]
    cols = [columns(pos_ref[3], local, p, 0, rows) for p in (x0_ref, x1_ref)]
    for j in range(local):
        for x_ref, sum_ref, col in ((x0_ref, o0_ref, cols[0]), (x1_ref, acc_ref, cols[1])):
            part = expert(x_ref[:rows, :], col[:, j:j + 1], g_ref[j], u_ref[j], d_ref[j])
            sum_ref[...] = part if j == 0 else sum_ref[...] + part
    o1_ref[...] = acc_ref[...].astype(BF16)


def far_open_kernel(local, at, span, pos_ref, x0_ref, x1_ref, g_ref, u_ref, d_ref, x_ref, col_ref, acc_ref):
    size = x_ref.shape[0] // 2
    x_ref[:size, :] = x0_ref[at:at + size, :]
    x_ref[size:, :] = x1_ref[at:at + size, :]
    cols = jnp.concatenate([columns(pos_ref[3], local, p, at, size) for p in (x0_ref, x1_ref)], axis=0)
    col_ref[...] = cols
    for j in span:
        part = expert(x_ref[...], cols[:, j:j + 1], g_ref[j], u_ref[j], d_ref[j])
        acc_ref[...] = part if j == 0 else acc_ref[...] + part


def far_close_kernel(span, x_ref, col_ref, sum_ref, g_ref, u_ref, d_ref, o0_ref, o1_ref, acc_ref):
    size = o0_ref.shape[0]
    for j in span:
        part = expert(x_ref[...], col_ref[:, j:j + 1], g_ref[j], u_ref[j], d_ref[j])
        acc_ref[...] = (sum_ref if j == span[0] else acc_ref)[...] + part
    o0_ref[...] = acc_ref[:size, :].astype(BF16)
    o1_ref[...] = acc_ref[size:, :].astype(BF16)


def far_kernel(local, at, pos_ref, x0_ref, x1_ref, g_ref, u_ref, d_ref, o0_ref, o1_ref, x_ref, col_ref,
               acc_ref):
    size = o0_ref.shape[0]
    far_open_kernel(local, at, range(local), pos_ref, x0_ref, x1_ref, g_ref, u_ref, d_ref, x_ref, col_ref,
                    acc_ref)
    o0_ref[...] = acc_ref[:size, :].astype(BF16)
    o1_ref[...] = acc_ref[size:, :].astype(BF16)


def add_kernel(a_ref, b_ref, o_ref):
    o_ref[...] = (a_ref[...].astype(F32) + b_ref[...].astype(F32)).astype(BF16)


def join_kernel(*refs):
    depth = refs[0].shape[0]
    for i, x_ref in enumerate(refs[:-1]):
        refs[-1][:, i * depth:(i + 1) * depth] = x_ref[...].T


def final_kernel(n_back, at, chunks, copies, depth, pos_ref, near_ref, core_ref, *refs):
    out_ref, block_ref, sem = refs[-3:]
    half, rep, core = pos_ref[1], pos_ref[2], pos_ref[0]
    size = block_ref.shape[1]
    total = near_ref[at:at + size, :] + core_ref[at:at + size, :].astype(F32)
    for s_ref in refs[:n_back]:
        total = total + s_ref[...].astype(F32)
    merged = total.astype(BF16)
    outs = []
    for i, ((c, b), w_ref) in enumerate(zip(chunks, refs[n_back:])):
        block_ref[i] = jnp.dot(merged, w_ref[...], preferred_element_type=F32).astype(BF16)
        for a in range(w_ref.shape[1] // depth):
            e = 2 * (half ^ a) + (core ^ c)
            to = pl.multiple_of((e * copies + (rep ^ b)) * depth, depth)
            outs.append(pltpu.make_async_copy(block_ref.at[i, :, pl.ds(a * depth, depth)],
                                              out_ref.at[pl.ds(at, size), pl.ds(to, depth)], sem.at[i, a]))
            outs[-1].start()
    for out in outs:
        out.wait()


def shape(dims, dtype=BF16):
    return jax.ShapeDtypeStruct(dims, dtype)


def on_device(tokens, norm_gain, router, down_proj, up_proj, expert_gate, expert_up, expert_down,
              expert_ids, slot_pos, overflow_list):
    rows, width = tokens.shape
    top = expert_ids.shape[1]
    local, _, ff = expert_gate.shape
    depth, latent = down_proj.shape
    groups = lax.axis_size("groups")
    shards = lax.axis_size("expert")
    copies = lax.axis_size("replica")
    chips = shards // 2
    wide = copies * depth
    spread = copies
    if depth % 128:
        down_proj = lax.all_gather(down_proj, "replica", axis=0, tiled=True)
        up_proj = lax.all_gather(up_proj, "replica", axis=0, tiled=True)
        depth, spread = wide, 1
    experts = shards * local
    g = lax.axis_index("groups")
    e = lax.axis_index("expert")
    r = lax.axis_index("replica")
    pos = jnp.stack([e % 2, e // 2, r if spread > 1 else 0 * r, e, g]).astype(jnp.int32)

    down = {(0, 0): down_proj}
    if spread == groups + 2 and groups == 2:
        near_z = swap(down_proj, "replica", 1)
        far_z = swap_pair(down_proj, ("groups", "replica"), lambda i, j: (i, j ^ (2 + i)))
        down[(0, 1)] = near_z
        down[(0, "A")] = far_z
        for a in range(1, chips):
            down[(a, 0)] = swap(down_proj, "expert", 2 * a)
        ups_x = [swap(up_proj, "expert", 2 * a) for a in range(1, chips)]
        for a in range(1, chips):
            down[(a, 1)] = swap(near_z, "expert", 2 * a)
            down[(a, "B")] = swap_pair(far_z, ("groups", "expert"),
                                       lambda i, j: (i ^ 1, j ^ (2 * a)))
            down[(a, "A")] = swap(far_z, "expert", 2 * a)
        down[(0, "B")] = swap(far_z, "groups", 1)
    else:
        for b in range(1, spread):
            down[(0, b)] = swap(down_proj, "replica", b)
        for b in range(spread):
            for a in range(1, chips):
                down[(a, b)] = swap(down[(0, b)], "expert", 2 * a)
        ups_x = [swap(up_proj, "expert", 2 * a) for a in range(1, chips)]

    keep, send, normed = kernel(
        functools.partial(norm_kernel, wide),
        (shape((rows, width // 2)), shape((rows, width // 2)), shape((rows, width))),
        (pos, in_hbm(tokens), in_hbm(norm_gain.reshape(1, width))), [SM] + [AN] * 2, 16,
        8 * rows * width, 4 * rows * width,
        [pltpu.VMEM((rows, width), BF16), pltpu.VMEM((1, width), F32), pltpu.SemaphoreType.DMA((2,))])
    recv = swap(send, "expert", 1)
    wt, own_down, own_up, last = kernel(
        functools.partial(gate_kernel, top),
        (shape((experts, rows), F32), shape(down_proj.shape), shape(up_proj.shape), shape(expert_down.shape)),
        (normed, *map(in_hbm, (overflow_list, router.T, expert_ids.T, slot_pos.T, down_proj, up_proj,
                               expert_down))),
        [VM] + [AN] * 7, 14, 4 * rows * width * experts, 4 * rows * width,
        [pltpu.SMEM(overflow_list.shape, jnp.int32), pltpu.VMEM((experts, width), BF16),
         pltpu.VMEM((top, rows), jnp.int32), pltpu.VMEM((top, rows), jnp.int32),
         pltpu.SemaphoreType.DMA((7,))])
    down[(0, 0)] = own_down
    weights = (expert_gate, expert_up, last)

    late = [k for k in down if (k[1] == "A" and k[0]) or k[1] == "B"] or list(down)[-1:]
    early = [k for k in down if k not in late]

    def scratch(n):
        return [pltpu.VMEM((2 * rows, n * depth), BF16), pltpu.VMEM((n * depth, latent), BF16)]

    opened = kernel(
        functools.partial(early_kernel, early, wide), shape((2 * rows, latent), F32),
        (pos, keep, recv, *[down[k] for k in early]), [SM] + [VM] * (2 + len(early)), 12,
        4 * rows * len(early) * depth * latent, 2 * len(early) * depth * latent, scratch(len(early)))
    partial = kernel(
        functools.partial(late_kernel, late, wide), shape((2 * rows + experts, latent), F32),
        (pos, keep, recv, opened, wt, *[down[k] for k in late]), [SM] + [VM] * (4 + len(late)), 12,
        4 * rows * len(late) * depth * latent, 2 * len(late) * depth * latent, scratch(len(late)))
    partial_core = swap(partial, "expert", 1)
    own, core = kernel(
        finish_kernel, (shape((rows + experts, latent)),) * 2, (partial, partial_core), [VM, VM],
        6, 2 * rows * latent, 12 * rows * latent)

    work = 6 * rows * latent * ff
    load = 6 * latent * ff
    far = []
    for a in range(1, chips):
        x0 = swap(own, "expert", 2 * a)
        far.append((x0, swap(x0, "expert", 1)))
    near0, near1 = kernel(
        functools.partial(near_kernel, local), (shape((rows, latent), F32), shape((rows, latent))),
        (pos, own, core, *weights), [SM] + [VM] * 5, 20, 2 * local * work, local * load,
        [pltpu.VMEM((rows, latent), F32)])
    near1 = swap(near1, "expert", 1)
    parts = 2
    size = rows // parts
    cut = local // 2
    back = [[], []]
    for a in range(1, chips):
        x = shape((2 * size, latent))
        col = shape((2 * size, local + -local % 8), F32)
        acc = shape((2 * size, latent), F32)
        out = (shape((size, latent)),) * 2
        o0, o1 = kernel(
            functools.partial(far_kernel, local, 0), out, (pos, *far[a - 1], *weights),
            [SM] + [VM] * 5, 20, local * work, local * load,
            [pltpu.VMEM(v.shape, v.dtype) for v in (x, col, acc)])
        results = [(o0, swap(o1, "expert", 1))]
        held = kernel(
            functools.partial(far_open_kernel, local, size, range(cut)), (x, col, acc),
            (pos, *far[a - 1], *weights), [SM] + [VM] * 5, 20, cut * work, cut * load)
        o0, o1 = kernel(
            functools.partial(far_close_kernel, range(cut, local)), out, (*held, *weights),
            [VM] * 6, 20, (local - cut) * work, (local - cut) * load, [pltpu.VMEM(acc.shape, F32)])
        results.append((o0, swap(o1, "expert", 1)))
        for h, pair in enumerate(results):
            s = kernel(add_kernel, shape((size, latent)), pair, [VM, VM], 4,
                       size * latent, 6 * size * latent)
            back[h].append(swap(s, "expert", 2 * a))

    pair = kernel(join_kernel, shape((latent, chips * depth)), (own_up, *ups_x),
                  [VM] * chips, 4, 0, 4 * chips * depth * latent)
    ups = {(0, 0): pair}
    for b in range(1, spread):
        ups[(0, b)] = swap(pair, "replica", b)
    for b in range(spread):
        ups[(1, b)] = swap(ups[(0, b)], "expert", 1)
    order = sorted(ups)
    result = None
    for h in range(parts):
        operands = (pos, near0, near1, *back[h], *[ups[k] for k in order])
        result = kernel(
            functools.partial(final_kernel, len(back[h]), h * size, order, spread, depth),
            shape((rows, width)), operands + ((result,) if h else ()),
            [SM] + [VM] * (len(operands) - 1) + [AN] * h, 10, 2 * size * width * latent, 2 * width * latent,
            [pltpu.VMEM((len(order), size, chips * depth), BF16),
             pltpu.SemaphoreType.DMA((len(order), chips))],
            AN, {len(operands): 0} if h else {})
    return result


def solution(mesh):
    placed = (
        P(("groups", "expert", "replica"), None),
        P(),
        P(),
        P(("expert", "replica"), None),
        P(("expert", "replica"), None),
        P("expert", None, None),
        P("expert", None, None),
        P("expert", None, None),
        P(("groups", "expert", "replica"), None),
        P(("groups", "expert", "replica"), None),
        P(("groups", "expert", "replica"), None, None, None),
    )

    return jax.shard_map(
        on_device,
        mesh=mesh,
        in_specs=placed,
        out_specs=P(("groups", "expert", "replica"), None),
        check_vma=False,
    )
```

```python
import functools

import jax
import jax.numpy as jnp
from jax import lax
from jax.experimental import pallas as pl
from jax.experimental.pallas import tpu as pltpu
from jax.sharding import PartitionSpec as P

epsilon = 1e-06
F32 = jnp.float32
BF16 = jnp.bfloat16

VM = pl.BlockSpec(memory_space=pltpu.VMEM)
SM = pl.BlockSpec(memory_space=pltpu.SMEM)
AN = pl.BlockSpec(memory_space=pl.ANY)


def in_hbm(x):
    return pltpu.with_memory_space_constraint(x, pltpu.HBM)


def swap(x, axis, bits):
    size = lax.axis_size(axis)
    return lax.ppermute(x, axis, [(i, i ^ bits) for i in range(size)])


def swap_pair(x, axes, move):
    sizes = [lax.axis_size(axis) for axis in axes]
    pairs = []
    for i in range(sizes[0]):
        for j in range(sizes[1]):
            p, q = move(i, j)
            pairs.append((i * sizes[1] + j, p * sizes[1] + q))
    return lax.ppermute(x, axes, pairs)


def kernel(body, out_shape, operands, specs, mib, flops=0, nbytes=0, scratch=(), out_specs=None,
           aliases={}):
    many = isinstance(out_shape, tuple)
    if out_specs is None:
        out_specs = (VM,) * len(out_shape) if many else VM
    return pl.pallas_call(
        body,
        out_shape=out_shape,
        in_specs=specs,
        out_specs=out_specs,
        scratch_shapes=list(scratch),
        input_output_aliases=aliases,
        compiler_params=pltpu.CompilerParams(vmem_limit_bytes=mib * 1024 * 1024),
        cost_estimate=pl.CostEstimate(flops=flops, bytes_accessed=nbytes, transcendentals=0),
    )(*operands)


def norm_kernel(pos_ref, tok_hbm, gain_hbm, normed_ref, tok_ref, gain_ref, sem):
    pairs = ((tok_hbm, tok_ref), (gain_hbm, gain_ref))
    copies = [pltpu.make_async_copy(src, dst, sem.at[i]) for i, (src, dst) in enumerate(pairs)]
    for copy in copies:
        copy.start()
    for copy in copies:
        copy.wait()
    values = tok_ref[...].astype(F32)
    scale = lax.rsqrt(jnp.mean(values * values, axis=-1, keepdims=True) + epsilon)
    normed_ref[...] = (values * scale * gain_ref[...]).astype(BF16)


def gate_kernel(top, normed_ref, list_hbm, router_hbm, ids_hbm, slot_hbm, down_hbm, up_hbm, last_hbm,
                wt_ref, down_ref, up_ref, last_ref, list_ref, router_ref, ids_ref, slot_ref, sem):
    pairs = ((router_hbm, router_ref), (ids_hbm, ids_ref), (slot_hbm, slot_ref), (list_hbm, list_ref),
             (up_hbm, up_ref), (down_hbm, down_ref), (last_hbm, last_ref))
    copies = [pltpu.make_async_copy(src, dst, sem.at[i]) for i, (src, dst) in enumerate(pairs)]
    for copy in copies:
        copy.start()
    for copy in copies[:4]:
        copy.wait()
    logits = lax.dot_general(router_ref[...], normed_ref[...], (((1,), (1,)), ((), ())),
                             preferred_element_type=F32)
    sig = jax.nn.sigmoid(logits)
    experts, rows = sig.shape
    sub = lax.broadcasted_iota(jnp.int32, (experts, rows), 0)
    lane = lax.broadcasted_iota(jnp.int32, (experts, rows), 1)
    total = jnp.zeros((experts, rows), F32)
    served = jnp.zeros((experts, rows), F32)
    for k in range(top):
        hit = sub == ids_ref[k:k + 1, :]
        total = total + jnp.where(hit, 1.0, 0.0)
        served = served + jnp.where(hit & (slot_ref[k:k + 1, :] >= 0), 1.0, 0.0)
    _, shards, copies_n, local = list_ref.shape

    def listed(i, served):
        shard, copy = i // copies_n, i % copies_n
        for m in range(local):
            entry = list_ref[0, shard, copy, m]
            owner = jnp.where(entry >= 0, entry, -top) // top
            served = served + jnp.where((lane == owner) & (sub == shard * local + m), 1.0, 0.0)
        return served

    served = lax.fori_loop(0, shards * copies_n, listed, served)
    denom = jnp.sum(total * sig, axis=0, keepdims=True)
    wt_ref[...] = jnp.where(served > 0.0, sig / denom, 0.0)
    for copy in copies[4:]:
        copy.wait()


def pile_kernel(*refs):
    depth = refs[0].shape[0]
    for i, x_ref in enumerate(refs[:-1]):
        refs[-1][i * depth:(i + 1) * depth, :] = x_ref[...]


def pick(chunks, other, depth, copies, pos_ref, normed_ref, x_ref):
    core, half, rep, group = pos_ref[0], pos_ref[1], pos_ref[2], pos_ref[4]
    for i, (a, b) in enumerate(chunks):
        if b == "A":
            b = 2 + group
        elif b == "B":
            b = 3 - group
        at = ((2 * (half ^ a) + (core ^ other)) * copies + (rep ^ b)) * depth
        x_ref[:, i * depth:(i + 1) * depth] = normed_ref[:, pl.ds(pl.multiple_of(at, depth), depth)]


def early_kernel(chunks, depth, copies, pos_ref, normed_ref, w0_ref, w1_ref, out_ref, x_ref):
    pick(chunks, 0, depth, copies, pos_ref, normed_ref, x_ref.at[0])
    pick(chunks, 1, depth, copies, pos_ref, normed_ref, x_ref.at[1])
    out_ref[...] = (jnp.dot(x_ref[0], w0_ref[...], preferred_element_type=F32)
                    + jnp.dot(x_ref[1], w1_ref[...], preferred_element_type=F32))


def late_kernel(chunks, copies, pos_ref, normed_ref, sum_ref, wt_ref, *refs):
    w_refs, (out_ref, x_ref, w_ref) = refs[:-3], refs[-3:]
    n = len(chunks)
    rows = normed_ref.shape[0]
    depth = w_refs[0].shape[0]
    for c in range(2):
        pick(chunks, c, depth, copies, pos_ref, normed_ref, x_ref.at[:, c * n * depth:(c + 1) * n * depth])
    for i, chunk in enumerate(w_refs):
        w_ref[i * depth:(i + 1) * depth, :] = chunk[...]
    out_ref[:rows, :] = (sum_ref[...] + jnp.dot(x_ref[...], w_ref[...],
                                                preferred_element_type=F32)).astype(BF16)
    wt = wt_ref[...]
    lead = wt.astype(BF16)
    out_ref[rows:, :rows] = lead
    out_ref[rows:, rows:] = (wt - lead.astype(F32)).astype(BF16)


def expert(x, weight, gate_w, up_w, down_w):
    gate = jnp.dot(x, gate_w, preferred_element_type=F32)
    upper = jnp.dot(x, up_w, preferred_element_type=F32)
    half = 0.5 * gate
    hidden = ((half + half * jnp.tanh(half)) * upper).astype(BF16)
    result = jnp.dot(hidden, down_w, preferred_element_type=F32).astype(BF16)
    return result.astype(F32) * weight


def columns(me, local, pay_ref, at, size):
    rows = pay_ref.shape[1] // 2
    wt = (pay_ref[rows:, at:at + size].astype(F32)
          + pay_ref[rows:, rows + at:rows + at + size].astype(F32))
    sub = lax.broadcasted_iota(jnp.int32, wt.shape, 0)
    picked = [jnp.sum(jnp.where(sub == me * local + j, wt, 0.0), axis=0, keepdims=True)
              for j in range(local)]
    pad = jnp.zeros((-local % 8, size), F32)
    return jnp.concatenate(picked + [pad], axis=0).T


def near_kernel(local, pos_ref, x0_ref, x1_ref, g_ref, u_ref, d_ref, o0_ref, o1_ref, acc_ref):
    rows = o0_ref.shape[0]
    cols = [columns(pos_ref[3], local, p, 0, rows) for p in (x0_ref, x1_ref)]
    for j in range(local):
        for x_ref, sum_ref, col in ((x0_ref, o0_ref, cols[0]), (x1_ref, acc_ref, cols[1])):
            part = expert(x_ref[:rows, :], col[:, j:j + 1], g_ref[j], u_ref[j], d_ref[j])
            sum_ref[...] = part if j == 0 else sum_ref[...] + part
    o1_ref[...] = acc_ref[...].astype(BF16)


def far_open_kernel(local, at, span, pos_ref, x0_ref, x1_ref, g_ref, u_ref, d_ref, x_ref, col_ref, acc_ref):
    size = x_ref.shape[0] // 2
    x_ref[:size, :] = x0_ref[at:at + size, :]
    x_ref[size:, :] = x1_ref[at:at + size, :]
    cols = jnp.concatenate([columns(pos_ref[3], local, p, at, size) for p in (x0_ref, x1_ref)], axis=0)
    col_ref[...] = cols
    for j in span:
        part = expert(x_ref[...], cols[:, j:j + 1], g_ref[j], u_ref[j], d_ref[j])
        acc_ref[...] = part if j == 0 else acc_ref[...] + part


def far_close_kernel(span, x_ref, col_ref, sum_ref, g_ref, u_ref, d_ref, o0_ref, o1_ref, acc_ref):
    size = o0_ref.shape[0]
    for j in span:
        part = expert(x_ref[...], col_ref[:, j:j + 1], g_ref[j], u_ref[j], d_ref[j])
        acc_ref[...] = (sum_ref if j == span[0] else acc_ref)[...] + part
    o0_ref[...] = acc_ref[:size, :].astype(BF16)
    o1_ref[...] = acc_ref[size:, :].astype(BF16)


def far_kernel(local, at, pos_ref, x0_ref, x1_ref, g_ref, u_ref, d_ref, o0_ref, o1_ref, x_ref, col_ref,
               acc_ref):
    size = o0_ref.shape[0]
    far_open_kernel(local, at, range(local), pos_ref, x0_ref, x1_ref, g_ref, u_ref, d_ref, x_ref, col_ref,
                    acc_ref)
    o0_ref[...] = acc_ref[:size, :].astype(BF16)
    o1_ref[...] = acc_ref[size:, :].astype(BF16)


def add_kernel(a_ref, b_ref, o_ref):
    o_ref[...] = (a_ref[...].astype(F32) + b_ref[...].astype(F32)).astype(BF16)


def join_kernel(*refs):
    depth = refs[0].shape[0]
    for i, x_ref in enumerate(refs[:-1]):
        refs[-1][:, i * depth:(i + 1) * depth] = x_ref[...].T


def final_kernel(n_back, at, chunks, copies, depth, pos_ref, near_ref, core_ref, *refs):
    out_ref, rows_ref, sem = refs[-3:]
    half, rep, core = pos_ref[1], pos_ref[2], pos_ref[0]
    size = rows_ref.shape[0]
    total = near_ref[at:at + size, :] + core_ref[at:at + size, :].astype(F32)
    for s_ref in refs[:n_back]:
        total = total + s_ref[...].astype(F32)
    merged = total.astype(BF16)
    for (c, b), w_ref in zip(chunks, refs[n_back:]):
        block = jnp.dot(merged, w_ref[...], preferred_element_type=F32).astype(BF16)
        for a in range(w_ref.shape[1] // depth):
            e = 2 * (half ^ a) + (core ^ c)
            to = pl.multiple_of((e * copies + (rep ^ b)) * depth, depth)
            rows_ref[:, pl.ds(to, depth)] = block[:, a * depth:(a + 1) * depth]
    out = pltpu.make_async_copy(rows_ref, out_ref.at[pl.ds(at, size), :], sem)
    out.start()
    out.wait()


def shape(dims, dtype=BF16):
    return jax.ShapeDtypeStruct(dims, dtype)


def on_device(tokens, norm_gain, router, down_proj, up_proj, expert_gate, expert_up, expert_down,
              expert_ids, slot_pos, overflow_list):
    rows, width = tokens.shape
    top = expert_ids.shape[1]
    local, _, ff = expert_gate.shape
    depth, latent = down_proj.shape
    groups = lax.axis_size("groups")
    shards = lax.axis_size("expert")
    copies = lax.axis_size("replica")
    chips = shards // 2
    wide = copies * depth
    spread = copies
    if depth % 128:
        down_proj = lax.all_gather(down_proj, "replica", axis=0, tiled=True)
        up_proj = lax.all_gather(up_proj, "replica", axis=0, tiled=True)
        depth, spread = wide, 1
    experts = shards * local
    g = lax.axis_index("groups")
    e = lax.axis_index("expert")
    r = lax.axis_index("replica")
    pos = jnp.stack([e % 2, e // 2, r if spread > 1 else 0 * r, e, g]).astype(jnp.int32)

    down = {(0, 0): down_proj}
    if spread == groups + 2 and groups == 2:
        near_z = swap(down_proj, "replica", 1)
        far_z = swap_pair(down_proj, ("groups", "replica"), lambda i, j: (i, j ^ (2 + i)))
        down[(0, 1)] = near_z
        down[(0, "A")] = far_z
        for a in range(1, chips):
            down[(a, 0)] = swap(down_proj, "expert", 2 * a)
        ups_x = [swap(up_proj, "expert", 2 * a) for a in range(1, chips)]
        for a in range(1, chips):
            down[(a, 1)] = swap(near_z, "expert", 2 * a)
            down[(a, "B")] = swap_pair(far_z, ("groups", "expert"),
                                       lambda i, j: (i ^ 1, j ^ (2 * a)))
            down[(a, "A")] = swap(far_z, "expert", 2 * a)
        down[(0, "B")] = swap(far_z, "groups", 1)
    else:
        for b in range(1, spread):
            down[(0, b)] = swap(down_proj, "replica", b)
        for b in range(spread):
            for a in range(1, chips):
                down[(a, b)] = swap(down[(0, b)], "expert", 2 * a)
        ups_x = [swap(up_proj, "expert", 2 * a) for a in range(1, chips)]

    normed = kernel(
        norm_kernel, shape((rows, width)), (pos, in_hbm(tokens), in_hbm(norm_gain.reshape(1, width))),
        [SM] + [AN] * 2, 16, 8 * rows * width, 4 * rows * width,
        [pltpu.VMEM((rows, width), BF16), pltpu.VMEM((1, width), F32), pltpu.SemaphoreType.DMA((2,))])
    wt, own_down, own_up, last = kernel(
        functools.partial(gate_kernel, top),
        (shape((experts, rows), F32), shape(down_proj.shape), shape(up_proj.shape), shape(expert_down.shape)),
        (normed, *map(in_hbm, (overflow_list, router.T, expert_ids.T, slot_pos.T, down_proj, up_proj,
                               expert_down))),
        [VM] + [AN] * 7, 14, 4 * rows * width * experts, 4 * rows * width,
        [pltpu.SMEM(overflow_list.shape, jnp.int32), pltpu.VMEM((experts, width), BF16),
         pltpu.VMEM((top, rows), jnp.int32), pltpu.VMEM((top, rows), jnp.int32),
         pltpu.SemaphoreType.DMA((7,))])
    down[(0, 0)] = own_down
    weights = (expert_gate, expert_up, last)

    late = [k for k in down if (k[1] == "A" and k[0]) or k[1] == "B"] or list(down)[-1:]
    early = [k for k in down if k not in late]

    n = len(early)
    stacked = kernel(pile_kernel, shape((n * depth, latent)), [down[k] for k in early], [VM] * n,
                     6, 0, 4 * n * depth * latent)
    stacked_core = swap(stacked, "expert", 1)
    late_core = [swap(down[k], "expert", 1) for k in late]
    opened = kernel(
        functools.partial(early_kernel, early, depth, spread), shape((rows, latent), F32),
        (pos, normed, stacked, stacked_core), [SM] + [VM] * 3, 10, 4 * rows * n * depth * latent,
        4 * n * depth * latent, [pltpu.VMEM((2, rows, n * depth), BF16)])
    n = len(late)
    own = kernel(
        functools.partial(late_kernel, late, spread), shape((rows + experts, latent)),
        (pos, normed, opened, wt, *[down[k] for k in late], *late_core), [SM] + [VM] * (3 + 2 * n), 10,
        4 * rows * n * depth * latent, 4 * n * depth * latent,
        [pltpu.VMEM((rows, 2 * n * depth), BF16), pltpu.VMEM((2 * n * depth, latent), BF16)])
    core = swap(own, "expert", 1)

    work = 6 * rows * latent * ff
    load = 6 * latent * ff
    far = []
    for a in range(1, chips):
        x0 = swap(own, "expert", 2 * a)
        far.append((x0, swap(x0, "expert", 1)))
    near0, near1 = kernel(
        functools.partial(near_kernel, local), (shape((rows, latent), F32), shape((rows, latent))),
        (pos, own, core, *weights), [SM] + [VM] * 5, 20, 2 * local * work, local * load,
        [pltpu.VMEM((rows, latent), F32)])
    near1 = swap(near1, "expert", 1)
    parts = 2
    size = rows // parts
    cut = local // 2
    back = [[], []]
    for a in range(1, chips):
        x = shape((2 * size, latent))
        col = shape((2 * size, local + -local % 8), F32)
        acc = shape((2 * size, latent), F32)
        out = (shape((size, latent)),) * 2
        o0, o1 = kernel(
            functools.partial(far_kernel, local, 0), out, (pos, *far[a - 1], *weights),
            [SM] + [VM] * 5, 20, local * work, local * load,
            [pltpu.VMEM(v.shape, v.dtype) for v in (x, col, acc)])
        results = [(o0, swap(o1, "expert", 1))]
        held = kernel(
            functools.partial(far_open_kernel, local, size, range(cut)), (x, col, acc),
            (pos, *far[a - 1], *weights), [SM] + [VM] * 5, 20, cut * work, cut * load)
        o0, o1 = kernel(
            functools.partial(far_close_kernel, range(cut, local)), out, (*held, *weights),
            [VM] * 6, 20, (local - cut) * work, (local - cut) * load, [pltpu.VMEM(acc.shape, F32)])
        results.append((o0, swap(o1, "expert", 1)))
        for h, pair in enumerate(results):
            s = kernel(add_kernel, shape((size, latent)), pair, [VM, VM], 4,
                       size * latent, 6 * size * latent)
            back[h].append(swap(s, "expert", 2 * a))

    pair = kernel(join_kernel, shape((latent, chips * depth)), (own_up, *ups_x),
                  [VM] * chips, 4, 0, 4 * chips * depth * latent)
    ups = {(0, 0): pair}
    for b in range(1, spread):
        ups[(0, b)] = swap(pair, "replica", b)
    for b in range(spread):
        ups[(1, b)] = swap(ups[(0, b)], "expert", 1)
    order = sorted(ups)
    result = None
    for h in range(parts):
        operands = (pos, near0, near1, *back[h], *[ups[k] for k in order])
        result = kernel(
            functools.partial(final_kernel, len(back[h]), h * size, order, spread, depth),
            shape((rows, width)), operands + ((result,) if h else ()),
            [SM] + [VM] * (len(operands) - 1) + [AN] * h, 10, 2 * size * width * latent, 2 * width * latent,
            [pltpu.VMEM((size, width), BF16), pltpu.SemaphoreType.DMA],
            AN, {len(operands): 0} if h else {})
    return result


def solution(mesh):
    placed = (
        P(("groups", "expert", "replica"), None),
        P(),
        P(),
        P(("expert", "replica"), None),
        P(("expert", "replica"), None),
        P("expert", None, None),
        P("expert", None, None),
        P("expert", None, None),
        P(("groups", "expert", "replica"), None),
        P(("groups", "expert", "replica"), None),
        P(("groups", "expert", "replica"), None, None, None),
    )

    return jax.shard_map(
        on_device,
        mesh=mesh,
        in_specs=placed,
        out_specs=P(("groups", "expert", "replica"), None),
        check_vma=False,
    )
```

```python
import functools

import jax
import jax.numpy as jnp
from jax import lax
from jax.experimental import pallas as pl
from jax.experimental.pallas import tpu as pltpu
from jax.sharding import PartitionSpec as P

epsilon = 1e-06
F32 = jnp.float32
BF16 = jnp.bfloat16

VM = pl.BlockSpec(memory_space=pltpu.VMEM)
AN = pl.BlockSpec(memory_space=pl.ANY)


def here(copies):
    e = lax.axis_index("expert")
    rep = lax.axis_index("replica") if copies > 1 else 0
    return lax.rem(e, 2), e // 2, rep, lax.axis_index("groups")


def in_hbm(x):
    return pltpu.with_memory_space_constraint(x, pltpu.HBM)


def swap(x, axis, bits):
    size = lax.axis_size(axis)
    return lax.ppermute(x, axis, [(i, i ^ bits) for i in range(size)])


def swap_pair(x, axes, move):
    sizes = [lax.axis_size(axis) for axis in axes]
    pairs = []
    for i in range(sizes[0]):
        for j in range(sizes[1]):
            p, q = move(i, j)
            pairs.append((i * sizes[1] + j, p * sizes[1] + q))
    return lax.ppermute(x, axes, pairs)


def kernel(body, out_shape, operands, specs, mib, flops=0, nbytes=0, scratch=(), out_specs=None,
           aliases={}):
    many = isinstance(out_shape, tuple)
    if out_specs is None:
        out_specs = (VM,) * len(out_shape) if many else VM
    return pl.pallas_call(
        body,
        out_shape=out_shape,
        in_specs=specs,
        out_specs=out_specs,
        scratch_shapes=list(scratch),
        input_output_aliases=aliases,
        compiler_params=pltpu.CompilerParams(vmem_limit_bytes=mib * 1024 * 1024),
        cost_estimate=pl.CostEstimate(flops=flops, bytes_accessed=nbytes, transcendentals=0),
    )(*operands)


def norm_kernel(tok_hbm, gain_hbm, normed_ref, tok_ref, gain_ref, sem):
    pairs = ((tok_hbm, tok_ref), (gain_hbm, gain_ref))
    copies = [pltpu.make_async_copy(src, dst, sem.at[i]) for i, (src, dst) in enumerate(pairs)]
    for copy in copies:
        copy.start()
    for copy in copies:
        copy.wait()
    values = tok_ref[...].astype(F32)
    scale = lax.rsqrt(jnp.mean(values * values, axis=-1, keepdims=True) + epsilon)
    normed_ref[...] = (values * scale * gain_ref[...]).astype(BF16)


def gate_kernel(top, normed_ref, list_hbm, router_hbm, ids_hbm, slot_hbm, down_hbm, up_hbm, last_hbm,
                wt_ref, down_ref, up_ref, last_ref, list_ref, router_ref, ids_ref, slot_ref, sem):
    pairs = ((router_hbm, router_ref), (ids_hbm, ids_ref), (slot_hbm, slot_ref), (list_hbm, list_ref),
             (up_hbm, up_ref), (down_hbm, down_ref), (last_hbm, last_ref))
    copies = [pltpu.make_async_copy(src, dst, sem.at[i]) for i, (src, dst) in enumerate(pairs)]
    for copy in copies:
        copy.start()
    for copy in copies[:4]:
        copy.wait()
    logits = lax.dot_general(router_ref[...], normed_ref[...], (((1,), (1,)), ((), ())),
                             preferred_element_type=F32)
    sig = jax.nn.sigmoid(logits)
    experts, rows = sig.shape
    sub = lax.broadcasted_iota(jnp.int32, (experts, rows), 0)
    lane = lax.broadcasted_iota(jnp.int32, (experts, rows), 1)
    total = jnp.zeros((experts, rows), F32)
    served = jnp.zeros((experts, rows), F32)
    for k in range(top):
        hit = sub == ids_ref[k:k + 1, :]
        total = total + jnp.where(hit, 1.0, 0.0)
        served = served + jnp.where(hit & (slot_ref[k:k + 1, :] >= 0), 1.0, 0.0)
    _, shards, copies_n, local = list_ref.shape

    def listed(i, served):
        shard, copy = i // copies_n, i % copies_n
        for m in range(local):
            entry = list_ref[0, shard, copy, m]
            owner = jnp.where(entry >= 0, entry, -top) // top
            served = served + jnp.where((lane == owner) & (sub == shard * local + m), 1.0, 0.0)
        return served

    served = lax.fori_loop(0, shards * copies_n, listed, served)
    denom = jnp.sum(total * sig, axis=0, keepdims=True)
    wt_ref[...] = jnp.where(served > 0.0, sig / denom, 0.0)
    for copy in copies[4:]:
        copy.wait()


def pile_kernel(*refs):
    depth = refs[0].shape[0]
    for i, x_ref in enumerate(refs[:-1]):
        refs[-1][i * depth:(i + 1) * depth, :] = x_ref[...]


def pick(chunks, other, depth, copies, normed_ref, x_ref):
    core, half, rep, group = here(copies)
    for i, (a, b) in enumerate(chunks):
        if b == "A":
            b = 2 + group
        elif b == "B":
            b = 3 - group
        at = ((2 * (half ^ a) + (core ^ other)) * copies + (rep ^ b)) * depth
        x_ref[:, i * depth:(i + 1) * depth] = normed_ref[:, pl.ds(pl.multiple_of(at, depth), depth)]


def early_kernel(chunks, depth, copies, normed_ref, w0_ref, w1_ref, out_ref, x_ref):
    pick(chunks, 0, depth, copies, normed_ref, x_ref.at[0])
    pick(chunks, 1, depth, copies, normed_ref, x_ref.at[1])
    out_ref[...] = (jnp.dot(x_ref[0], w0_ref[...], preferred_element_type=F32)
                    + jnp.dot(x_ref[1], w1_ref[...], preferred_element_type=F32))


def late_kernel(chunks, copies, normed_ref, sum_ref, wt_ref, *refs):
    w_refs, (out_ref, x_ref, w_ref) = refs[:-3], refs[-3:]
    n = len(chunks)
    rows = normed_ref.shape[0]
    depth = w_refs[0].shape[0]
    for c in range(2):
        pick(chunks, c, depth, copies, normed_ref, x_ref.at[:, c * n * depth:(c + 1) * n * depth])
    for i, chunk in enumerate(w_refs):
        w_ref[i * depth:(i + 1) * depth, :] = chunk[...]
    out_ref[:rows, :] = (sum_ref[...] + jnp.dot(x_ref[...], w_ref[...],
                                                preferred_element_type=F32)).astype(BF16)
    wt = wt_ref[...]
    lead = wt.astype(BF16)
    out_ref[rows:, :rows] = lead
    out_ref[rows:, rows:] = (wt - lead.astype(F32)).astype(BF16)


def expert(x, weight, gate_w, up_w, down_w):
    gate = jnp.dot(x, gate_w, preferred_element_type=F32)
    upper = jnp.dot(x, up_w, preferred_element_type=F32)
    half = 0.5 * gate
    hidden = ((half + half * jnp.tanh(half)) * upper).astype(BF16)
    result = jnp.dot(hidden, down_w, preferred_element_type=F32).astype(BF16)
    return result.astype(F32) * weight


def columns(me, local, pay_ref, at, size):
    rows = pay_ref.shape[1] // 2
    wt = (pay_ref[rows:, at:at + size].astype(F32)
          + pay_ref[rows:, rows + at:rows + at + size].astype(F32))
    sub = lax.broadcasted_iota(jnp.int32, wt.shape, 0)
    picked = [jnp.sum(jnp.where(sub == (me ^ c) * local + j, wt, 0.0), axis=0, keepdims=True)
              for c in range(2) for j in range(local)]
    pad = [jnp.zeros((-len(picked) % 8, size), F32)] if len(picked) % 8 else []
    return jnp.concatenate(picked + pad, axis=0).T


def run_experts(span, at, size, pay_ref, w_refs, out_ref, start_ref=None):
    local = w_refs[0].shape[0]
    cols = columns(lax.axis_index("expert"), local, pay_ref, at, size)
    x = pay_ref[at:at + size, :]
    for j in span:
        refs = w_refs[:3] if j < local else w_refs[3:]
        part = expert(x, cols[:, j:j + 1], *(ref[j % local] for ref in refs))
        if j == span[0]:
            out_ref[...] = part if start_ref is None else start_ref[at:at + size, :] + part
        else:
            out_ref[...] += part


def near_kernel(span, pay_ref, *refs):
    run_experts(span, 0, refs[-1].shape[0], pay_ref, refs[:6], refs[-1])


def far_kernel(span, at, pay_ref, sum_ref, *refs):
    out_ref, acc_ref = refs[-2:]
    run_experts(span, at, out_ref.shape[0], pay_ref, refs[:6], acc_ref, sum_ref)
    out_ref[...] = acc_ref[...].astype(BF16)


def join_kernel(*refs):
    depth = refs[0].shape[0]
    for i, x_ref in enumerate(refs[:-1]):
        refs[-1][:, i * depth:(i + 1) * depth] = x_ref[...].T


def final_kernel(n_back, at, chunks, copies, depth, near_ref, *refs):
    out_ref, rows_ref, sem = refs[-3:]
    core, half, rep, _ = here(copies)
    size = rows_ref.shape[0]
    total = near_ref[at:at + size, :]
    for s_ref in refs[:n_back]:
        total = total + s_ref[...].astype(F32)
    merged = total.astype(BF16)
    for (c, b), w_ref in zip(chunks, refs[n_back:]):
        block = jnp.dot(merged, w_ref[...], preferred_element_type=F32).astype(BF16)
        for a in range(w_ref.shape[1] // depth):
            e = 2 * (half ^ a) + (core ^ c)
            to = pl.multiple_of((e * copies + (rep ^ b)) * depth, depth)
            rows_ref[:, pl.ds(to, depth)] = block[:, a * depth:(a + 1) * depth]
    out = pltpu.make_async_copy(rows_ref, out_ref.at[pl.ds(at, size), :], sem)
    out.start()
    out.wait()


def shape(dims, dtype=BF16):
    return jax.ShapeDtypeStruct(dims, dtype)


def on_device(tokens, norm_gain, router, down_proj, up_proj, expert_gate, expert_up, expert_down,
              expert_ids, slot_pos, overflow_list):
    rows, width = tokens.shape
    top = expert_ids.shape[1]
    local, _, ff = expert_gate.shape
    depth, latent = down_proj.shape
    groups = lax.axis_size("groups")
    shards = lax.axis_size("expert")
    copies = lax.axis_size("replica")
    chips = shards // 2
    wide = copies * depth
    spread = copies
    if depth % 128:
        down_proj = lax.all_gather(down_proj, "replica", axis=0, tiled=True)
        up_proj = lax.all_gather(up_proj, "replica", axis=0, tiled=True)
        depth, spread = wide, 1
    experts = shards * local
    down = {(0, 0): down_proj}
    if spread == groups + 2 and groups == 2:
        near_z = swap(down_proj, "replica", 1)
        far_z = swap_pair(down_proj, ("groups", "replica"), lambda i, j: (i, j ^ (2 + i)))
        down[(0, 1)] = near_z
        down[(0, "A")] = far_z
        for a in range(1, chips):
            down[(a, 0)] = swap(down_proj, "expert", 2 * a)
        ups_x = [swap(up_proj, "expert", 2 * a) for a in range(1, chips)]
        for a in range(1, chips):
            down[(a, 1)] = swap(near_z, "expert", 2 * a)
            down[(a, "B")] = swap_pair(far_z, ("groups", "expert"),
                                       lambda i, j: (i ^ 1, j ^ (2 * a)))
            down[(a, "A")] = swap(far_z, "expert", 2 * a)
        down[(0, "B")] = swap(far_z, "groups", 1)
    else:
        for b in range(1, spread):
            down[(0, b)] = swap(down_proj, "replica", b)
        for b in range(spread):
            for a in range(1, chips):
                down[(a, b)] = swap(down[(0, b)], "expert", 2 * a)
        ups_x = [swap(up_proj, "expert", 2 * a) for a in range(1, chips)]

    normed = kernel(
        norm_kernel, shape((rows, width)), (in_hbm(tokens), in_hbm(norm_gain.reshape(1, width))),
        [AN] * 2, 16, 8 * rows * width, 4 * rows * width,
        [pltpu.VMEM((rows, width), BF16), pltpu.VMEM((1, width), F32), pltpu.SemaphoreType.DMA((2,))])
    wt, own_down, own_up, last = kernel(
        functools.partial(gate_kernel, top),
        (shape((experts, rows), F32), shape(down_proj.shape), shape(up_proj.shape), shape(expert_down.shape)),
        (normed, *map(in_hbm, (overflow_list, router.T, expert_ids.T, slot_pos.T, down_proj, up_proj,
                               expert_down))),
        [VM] + [AN] * 7, 14, 4 * rows * width * experts, 4 * rows * width,
        [pltpu.SMEM(overflow_list.shape, jnp.int32), pltpu.VMEM((experts, width), BF16),
         pltpu.VMEM((top, rows), jnp.int32), pltpu.VMEM((top, rows), jnp.int32),
         pltpu.SemaphoreType.DMA((7,))])
    down[(0, 0)] = own_down
    weights = (expert_gate, expert_up, last, *[
        swap(w, "expert", 1) for w in (expert_gate, expert_up, expert_down)])

    late = [k for k in down if (k[1] == "A" and k[0]) or k[1] == "B"] or list(down)[-1:]
    early = [k for k in down if k not in late]

    n = len(early)
    stacked = kernel(pile_kernel, shape((n * depth, latent)), [down[k] for k in early], [VM] * n,
                     6, 0, 4 * n * depth * latent)
    stacked_core = swap(stacked, "expert", 1)
    late_core = [swap(down[k], "expert", 1) for k in late]
    opened = kernel(
        functools.partial(early_kernel, early, depth, spread), shape((rows, latent), F32),
        (normed, stacked, stacked_core), [VM] * 3, 10, 4 * rows * n * depth * latent,
        4 * n * depth * latent, [pltpu.VMEM((2, rows, n * depth), BF16)])
    n = len(late)
    own = kernel(
        functools.partial(late_kernel, late, spread), shape((rows + experts, latent)),
        (normed, opened, wt, *[down[k] for k in late], *late_core), [VM] * (3 + 2 * n), 10,
        4 * rows * n * depth * latent, 4 * n * depth * latent,
        [pltpu.VMEM((rows, 2 * n * depth), BF16), pltpu.VMEM((2 * n * depth, latent), BF16)])
    work = 6 * rows * latent * ff
    load = 6 * latent * ff
    count = 2 * local
    cut = count - local // 2
    far = [swap(own, "expert", 2 * a) for a in range(1, chips)]

    def run(payload, span):
        return kernel(
            functools.partial(near_kernel, span), shape((rows, latent), F32), (payload, *weights),
            [VM] * 7, 16, len(span) * work, len(span) * load)

    near = run(own, range(count))
    parts = 2
    size = rows // parts
    back = [[] for _ in range(parts)]
    for a in range(1, chips):
        opened = run(far[a - 1], range(cut))
        for h in range(parts):
            s = kernel(
                functools.partial(far_kernel, range(cut, count), h * size),
                shape((size, latent)), (far[a - 1], opened, *weights), [VM] * 8, 14,
                (count - cut) * work // parts, (count - cut) * load, [pltpu.VMEM((size, latent), F32)])
            back[h].append(swap(s, "expert", 2 * a))

    pair = kernel(join_kernel, shape((latent, chips * depth)), (own_up, *ups_x),
                  [VM] * chips, 4, 0, 4 * chips * depth * latent)
    ups = {(0, 0): pair}
    for b in range(1, spread):
        ups[(0, b)] = swap(pair, "replica", b)
    for b in range(spread):
        ups[(1, b)] = swap(ups[(0, b)], "expert", 1)
    order = sorted(ups)
    result = None
    for h in range(parts):
        operands = (near, *back[h], *[ups[k] for k in order])
        result = kernel(
            functools.partial(final_kernel, len(back[h]), h * size, order, spread, depth),
            shape((rows, width)), operands + ((result,) if h else ()),
            [VM] * len(operands) + [AN] * h, 10, 2 * size * width * latent, 2 * width * latent,
            [pltpu.VMEM((size, width), BF16), pltpu.SemaphoreType.DMA],
            AN, {len(operands): 0} if h else {})
    return result


def solution(mesh):
    placed = (
        P(("groups", "expert", "replica"), None),
        P(),
        P(),
        P(("expert", "replica"), None),
        P(("expert", "replica"), None),
        P("expert", None, None),
        P("expert", None, None),
        P("expert", None, None),
        P(("groups", "expert", "replica"), None),
        P(("groups", "expert", "replica"), None),
        P(("groups", "expert", "replica"), None, None, None),
    )

    return jax.shard_map(
        on_device,
        mesh=mesh,
        in_specs=placed,
        out_specs=P(("groups", "expert", "replica"), None),
        check_vma=False,
    )
```

```python
import functools

import jax
import jax.numpy as jnp
from jax import lax
from jax.experimental import pallas as pl
from jax.experimental.pallas import tpu as pltpu
from jax.sharding import PartitionSpec as P

epsilon = 1e-06
F32 = jnp.float32
BF16 = jnp.bfloat16

VM = pl.BlockSpec(memory_space=pltpu.VMEM)
AN = pl.BlockSpec(memory_space=pl.ANY)


def here(copies):
    e = lax.axis_index("expert")
    rep = lax.axis_index("replica") if copies > 1 else 0
    return lax.rem(e, 2), e // 2, rep, lax.axis_index("groups")


def in_hbm(x):
    return pltpu.with_memory_space_constraint(x, pltpu.HBM)


def swap(x, axis, bits):
    size = lax.axis_size(axis)
    return lax.ppermute(x, axis, [(i, i ^ bits) for i in range(size)])


def swap_pair(x, axes, move):
    sizes = [lax.axis_size(axis) for axis in axes]
    pairs = []
    for i in range(sizes[0]):
        for j in range(sizes[1]):
            p, q = move(i, j)
            pairs.append((i * sizes[1] + j, p * sizes[1] + q))
    return lax.ppermute(x, axes, pairs)


def kernel(body, out_shape, operands, specs, mib, flops=0, nbytes=0, scratch=(), out_specs=None,
           aliases={}):
    many = isinstance(out_shape, tuple)
    if out_specs is None:
        out_specs = (VM,) * len(out_shape) if many else VM
    return pl.pallas_call(
        body,
        out_shape=out_shape,
        in_specs=specs,
        out_specs=out_specs,
        scratch_shapes=list(scratch),
        input_output_aliases=aliases,
        compiler_params=pltpu.CompilerParams(vmem_limit_bytes=mib * 1024 * 1024),
        cost_estimate=pl.CostEstimate(flops=flops, bytes_accessed=nbytes, transcendentals=0),
    )(*operands)


def norm_kernel(tok_hbm, gain_hbm, down_hbm, up_hbm, normed_ref, down_ref, up_ref, tok_ref, gain_ref, sem):
    pairs = ((tok_hbm, tok_ref), (gain_hbm, gain_ref), (down_hbm, down_ref), (up_hbm, up_ref))
    copies = [pltpu.make_async_copy(src, dst, sem.at[i]) for i, (src, dst) in enumerate(pairs)]
    for copy in copies:
        copy.start()
    for copy in copies[:2]:
        copy.wait()
    values = tok_ref[...].astype(F32)
    scale = lax.rsqrt(jnp.mean(values * values, axis=-1, keepdims=True) + epsilon)
    normed_ref[...] = (values * scale * gain_ref[...]).astype(BF16)
    for copy in copies[2:]:
        copy.wait()


def gate_kernel(top, normed_ref, list_hbm, router_hbm, ids_hbm, slot_hbm, last_hbm, wt_ref, last_ref,
                list_ref, router_ref, ids_ref, slot_ref, sem):
    pairs = ((router_hbm, router_ref), (ids_hbm, ids_ref), (slot_hbm, slot_ref), (list_hbm, list_ref),
             (last_hbm, last_ref))
    copies = [pltpu.make_async_copy(src, dst, sem.at[i]) for i, (src, dst) in enumerate(pairs)]
    for copy in copies:
        copy.start()
    for copy in copies[:4]:
        copy.wait()
    logits = lax.dot_general(router_ref[...], normed_ref[...], (((1,), (1,)), ((), ())),
                             preferred_element_type=F32)
    sig = jax.nn.sigmoid(logits)
    experts, rows = sig.shape
    sub = lax.broadcasted_iota(jnp.int32, (experts, rows), 0)
    lane = lax.broadcasted_iota(jnp.int32, (experts, rows), 1)
    total = jnp.zeros((experts, rows), F32)
    served = jnp.zeros((experts, rows), F32)
    for k in range(top):
        hit = sub == ids_ref[k:k + 1, :]
        total = total + jnp.where(hit, 1.0, 0.0)
        served = served + jnp.where(hit & (slot_ref[k:k + 1, :] >= 0), 1.0, 0.0)
    _, shards, copies_n, local = list_ref.shape

    def listed(i, served):
        shard, copy = i // copies_n, i % copies_n
        for m in range(local):
            entry = list_ref[0, shard, copy, m]
            owner = jnp.where(entry >= 0, entry, -top) // top
            served = served + jnp.where((lane == owner) & (sub == shard * local + m), 1.0, 0.0)
        return served

    served = lax.fori_loop(0, shards * copies_n, listed, served)
    denom = jnp.sum(total * sig, axis=0, keepdims=True)
    wt_ref[...] = jnp.where(served > 0.0, sig / denom, 0.0)
    for copy in copies[4:]:
        copy.wait()


def pile_kernel(*refs):
    depth = refs[0].shape[0]
    for i, x_ref in enumerate(refs[:-1]):
        refs[-1][i * depth:(i + 1) * depth, :] = x_ref[...]


def pick(chunks, other, depth, copies, normed_ref, x_ref):
    core, half, rep, group = here(copies)
    for i, (a, b) in enumerate(chunks):
        b = {"A": 2 + group, "B": 3 - group}.get(b, b)
        at = ((2 * (half ^ a) + (core ^ other)) * copies + (rep ^ b)) * depth
        x_ref[:, i * depth:(i + 1) * depth] = normed_ref[:, pl.ds(pl.multiple_of(at, depth), depth)]


def early_kernel(chunks, depth, copies, normed_ref, w0_ref, w1_ref, out_ref, x_ref):
    pick(chunks, 0, depth, copies, normed_ref, x_ref.at[0])
    pick(chunks, 1, depth, copies, normed_ref, x_ref.at[1])
    out_ref[...] = (jnp.dot(x_ref[0], w0_ref[...], preferred_element_type=F32)
                    + jnp.dot(x_ref[1], w1_ref[...], preferred_element_type=F32))


def late_kernel(chunks, copies, normed_ref, sum_ref, wt_ref, *refs):
    w_refs, (out_ref, x_ref, w_ref) = refs[:-3], refs[-3:]
    n = len(chunks)
    rows = normed_ref.shape[0]
    depth = w_refs[0].shape[0]
    for c in range(2):
        pick(chunks, c, depth, copies, normed_ref, x_ref.at[:, c * n * depth:(c + 1) * n * depth])
    for i, chunk in enumerate(w_refs):
        w_ref[i * depth:(i + 1) * depth, :] = chunk[...]
    out_ref[:rows, :] = (sum_ref[...] + jnp.dot(x_ref[...], w_ref[...],
                                                preferred_element_type=F32)).astype(BF16)
    wt = wt_ref[...]
    lead = wt.astype(BF16)
    out_ref[rows:, :rows] = lead
    out_ref[rows:, rows:] = (wt - lead.astype(F32)).astype(BF16)


def expert(x, weight, gate_w, up_w, down_w):
    gate = jnp.dot(x, gate_w, preferred_element_type=F32)
    upper = jnp.dot(x, up_w, preferred_element_type=F32)
    half = 0.5 * gate
    hidden = ((half + half * jnp.tanh(half)) * upper).astype(BF16)
    result = jnp.dot(hidden, down_w, preferred_element_type=F32).astype(BF16)
    return result.astype(F32) * weight


def columns(me, local, pay_ref, at, size):
    rows = pay_ref.shape[1] // 2
    wt = (pay_ref[rows:, at:at + size].astype(F32)
          + pay_ref[rows:, rows + at:rows + at + size].astype(F32))
    sub = lax.broadcasted_iota(jnp.int32, wt.shape, 0)
    picked = [jnp.sum(jnp.where(sub == (me ^ c) * local + j, wt, 0.0), axis=0, keepdims=True)
              for c in range(2) for j in range(local)]
    pad = [jnp.zeros((-len(picked) % 8, size), F32)] if len(picked) % 8 else []
    return jnp.concatenate(picked + pad, axis=0).T


def run_experts(span, at, size, pay_ref, w_refs, out_ref, start_ref=None):
    local = w_refs[0].shape[0]
    cols = columns(lax.axis_index("expert"), local, pay_ref, at, size)
    x = pay_ref[at:at + size, :]
    for j in span:
        refs = w_refs[:3] if j < local else w_refs[3:]
        part = expert(x, cols[:, j:j + 1], *(ref[j % local] for ref in refs))
        if j == span[0]:
            out_ref[...] = part if start_ref is None else start_ref[at:at + size, :] + part
        else:
            out_ref[...] += part


def near_kernel(span, pay_ref, *refs):
    run_experts(span, 0, refs[-1].shape[0], pay_ref, refs[:6], refs[-1])


def far_kernel(span, at, pay_ref, sum_ref, *refs):
    out_ref, acc_ref = refs[-2:]
    run_experts(span, at, out_ref.shape[0], pay_ref, refs[:6], acc_ref, sum_ref)
    out_ref[...] = acc_ref[...].astype(BF16)


def join_kernel(*refs):
    depth = refs[0].shape[0]
    for i, x_ref in enumerate(refs[:-1]):
        refs[-1][:, i * depth:(i + 1) * depth] = x_ref[...].T


def final_kernel(n_back, at, chunks, copies, depth, near_ref, *refs):
    out_ref, rows_ref, sem = refs[-3:]
    core, half, rep, group = here(copies)
    size = rows_ref.shape[0]
    total = near_ref[at:at + size, :]
    for s_ref in refs[:n_back]:
        total = total + s_ref[...].astype(F32)
    merged = total.astype(BF16)
    for (c, b), w_ref in zip(chunks, refs[n_back:]):
        b = {"A": 2 + group, "B": 3 - group}.get(b, b)
        block = jnp.dot(merged, w_ref[...], preferred_element_type=F32).astype(BF16)
        for a in range(w_ref.shape[1] // depth):
            e = 2 * (half ^ a) + (core ^ c)
            to = pl.multiple_of((e * copies + (rep ^ b)) * depth, depth)
            rows_ref[:, pl.ds(to, depth)] = block[:, a * depth:(a + 1) * depth]
    out = pltpu.make_async_copy(rows_ref, out_ref.at[pl.ds(at, size), :], sem)
    out.start()
    out.wait()


def shape(dims, dtype=BF16):
    return jax.ShapeDtypeStruct(dims, dtype)


def on_device(tokens, norm_gain, router, down_proj, up_proj, expert_gate, expert_up, expert_down,
              expert_ids, slot_pos, overflow_list):
    rows, width = tokens.shape
    top = expert_ids.shape[1]
    local, _, ff = expert_gate.shape
    depth, latent = down_proj.shape
    groups = lax.axis_size("groups")
    shards = lax.axis_size("expert")
    copies = lax.axis_size("replica")
    chips = shards // 2
    wide = copies * depth
    spread = copies
    if depth % 128:
        down_proj = lax.all_gather(down_proj, "replica", axis=0, tiled=True)
        up_proj = lax.all_gather(up_proj, "replica", axis=0, tiled=True)
        depth, spread = wide, 1
    experts = shards * local
    down = {(0, 0): down_proj}
    far_z = None
    if spread == groups + 2 and groups == 2:
        near_z = swap(down_proj, "replica", 1)
        far_z = swap_pair(down_proj, ("groups", "replica"), lambda i, j: (i, j ^ (2 + i)))
        down[(0, 1)] = near_z
        down[(0, "A")] = far_z
        for a in range(1, chips):
            down[(a, 0)] = swap(down_proj, "expert", 2 * a)
        ups_x = [swap(up_proj, "expert", 2 * a) for a in range(1, chips)]
        for a in range(1, chips):
            down[(a, 1)] = swap(near_z, "expert", 2 * a)
            down[(a, "B")] = swap_pair(far_z, ("groups", "expert"),
                                       lambda i, j: (i ^ 1, j ^ (2 * a)))
            down[(a, "A")] = swap(far_z, "expert", 2 * a)
        down[(0, "B")] = swap(far_z, "groups", 1)
    else:
        for b in range(1, spread):
            down[(0, b)] = swap(down_proj, "replica", b)
        for b in range(spread):
            for a in range(1, chips):
                down[(a, b)] = swap(down[(0, b)], "expert", 2 * a)
        ups_x = [swap(up_proj, "expert", 2 * a) for a in range(1, chips)]

    normed, own_down, own_up = kernel(
        norm_kernel, (shape((rows, width)), shape(down_proj.shape), shape(up_proj.shape)),
        tuple(map(in_hbm, (tokens, norm_gain.reshape(1, width), down_proj, up_proj))),
        [AN] * 4, 16, 8 * rows * width, 4 * rows * width,
        [pltpu.VMEM((rows, width), BF16), pltpu.VMEM((1, width), F32), pltpu.SemaphoreType.DMA((4,))])
    wt, last = kernel(
        functools.partial(gate_kernel, top),
        (shape((experts, rows), F32), shape(expert_down.shape)),
        (normed, *map(in_hbm, (overflow_list, router.T, expert_ids.T, slot_pos.T, expert_down))),
        [VM] + [AN] * 5, 14, 4 * rows * width * experts, 4 * rows * width,
        [pltpu.SMEM(overflow_list.shape, jnp.int32), pltpu.VMEM((experts, width), BF16),
         pltpu.VMEM((top, rows), jnp.int32), pltpu.VMEM((top, rows), jnp.int32),
         pltpu.SemaphoreType.DMA((5,))])
    down[(0, 0)] = own_down
    weights = (expert_gate, expert_up, last, *[
        swap(w, "expert", 1) for w in (expert_gate, expert_up, expert_down)])

    late = [k for k in down if (k[1] == "A" and k[0]) or k[1] == "B"] or list(down)[-1:]
    early = [k for k in down if k not in late]

    n = len(early)
    stacked = kernel(pile_kernel, shape((n * depth, latent)), [down[k] for k in early], [VM] * n,
                     6, 0, 4 * n * depth * latent)
    stacked_core = swap(stacked, "expert", 1)
    late_core = [swap(down[k], "expert", 1) for k in late]
    opened = kernel(
        functools.partial(early_kernel, early, depth, spread), shape((rows, latent), F32),
        (normed, stacked, stacked_core), [VM] * 3, 10, 4 * rows * n * depth * latent,
        4 * n * depth * latent, [pltpu.VMEM((2, rows, n * depth), BF16)])
    n = len(late)
    own = kernel(
        functools.partial(late_kernel, late, spread), shape((rows + experts, latent)),
        (normed, opened, wt, *[down[k] for k in late], *late_core), [VM] * (3 + 2 * n), 10,
        4 * rows * n * depth * latent, 4 * n * depth * latent,
        [pltpu.VMEM((rows, 2 * n * depth), BF16), pltpu.VMEM((2 * n * depth, latent), BF16)])
    work = 6 * rows * latent * ff
    load = 6 * latent * ff
    count = 2 * local
    cut = count - local // 2
    far = [swap(own, "expert", 2 * a) for a in range(1, chips)]

    def run(payload, span):
        return kernel(
            functools.partial(near_kernel, span), shape((rows, latent), F32), (payload, *weights),
            [VM] * 7, 16, len(span) * work, len(span) * load)

    near = run(own, range(count))
    parts = 2
    size = rows // parts
    back = [[] for _ in range(parts)]
    for a in range(1, chips):
        opened = run(far[a - 1], range(cut))
        for h in range(parts):
            s = kernel(
                functools.partial(far_kernel, range(cut, count), h * size),
                shape((size, latent)), (far[a - 1], opened, *weights), [VM] * 8, 14,
                (count - cut) * work // parts, (count - cut) * load, [pltpu.VMEM((size, latent), F32)])
            back[h].append(swap(s, "expert", 2 * a))

    pair = kernel(join_kernel, shape((latent, chips * depth)), (own_up, *ups_x),
                  [VM] * chips, 4, 0, 4 * chips * depth * latent)
    ups = {(0, 0): pair}
    if far_z is not None:
        ups[(0, 1)] = swap(pair, "replica", 1)
        ups[(0, "A")] = swap_pair(pair, ("groups", "replica"), lambda i, j: (i, j ^ (2 + i)))
        ups[(0, "B")] = swap(ups[(0, "A")], "groups", 1)
    else:
        for b in range(1, spread):
            ups[(0, b)] = swap(pair, "replica", b)
    for _, b in list(ups):
        ups[(1, b)] = swap(ups[(0, b)], "expert", 1)
    order = list(ups)
    result = None
    for h in range(parts):
        operands = (near, *back[h], *[ups[k] for k in order])
        result = kernel(
            functools.partial(final_kernel, len(back[h]), h * size, order, spread, depth),
            shape((rows, width)), operands + ((result,) if h else ()),
            [VM] * len(operands) + [AN] * h, 10, 2 * size * width * latent, 2 * width * latent,
            [pltpu.VMEM((size, width), BF16), pltpu.SemaphoreType.DMA],
            AN, {len(operands): 0} if h else {})
    return result


def solution(mesh):
    placed = (
        P(("groups", "expert", "replica"), None),
        P(),
        P(),
        P(("expert", "replica"), None),
        P(("expert", "replica"), None),
        P("expert", None, None),
        P("expert", None, None),
        P("expert", None, None),
        P(("groups", "expert", "replica"), None),
        P(("groups", "expert", "replica"), None),
        P(("groups", "expert", "replica"), None, None, None),
    )

    return jax.shard_map(
        on_device,
        mesh=mesh,
        in_specs=placed,
        out_specs=P(("groups", "expert", "replica"), None),
        check_vma=False,
    )
```

```python
import functools

import jax
import jax.numpy as jnp
from jax import lax
from jax.experimental import pallas as pl
from jax.experimental.pallas import tpu as pltpu
from jax.sharding import PartitionSpec as P

epsilon = 1e-06
F32 = jnp.float32
BF16 = jnp.bfloat16

VM = pl.BlockSpec(memory_space=pltpu.VMEM)
AN = pl.BlockSpec(memory_space=pl.ANY)


def here(copies):
    e = lax.axis_index("expert")
    rep = lax.axis_index("replica") if copies > 1 else 0
    return lax.rem(e, 2), e // 2, rep, lax.axis_index("groups")


def in_hbm(x):
    return pltpu.with_memory_space_constraint(x, pltpu.HBM)


def swap(x, axis, bits):
    size = lax.axis_size(axis)
    return lax.ppermute(x, axis, [(i, i ^ bits) for i in range(size)])


def swap_pair(x, axes, move):
    sizes = [lax.axis_size(axis) for axis in axes]
    pairs = []
    for i in range(sizes[0]):
        for j in range(sizes[1]):
            p, q = move(i, j)
            pairs.append((i * sizes[1] + j, p * sizes[1] + q))
    return lax.ppermute(x, axes, pairs)


def kernel(body, out_shape, operands, specs, mib, flops=0, nbytes=0, scratch=(), out_specs=None,
           aliases={}):
    many = isinstance(out_shape, tuple)
    if out_specs is None:
        out_specs = (VM,) * len(out_shape) if many else VM
    return pl.pallas_call(
        body,
        out_shape=out_shape,
        in_specs=specs,
        out_specs=out_specs,
        scratch_shapes=list(scratch),
        input_output_aliases=aliases,
        compiler_params=pltpu.CompilerParams(vmem_limit_bytes=mib * 1024 * 1024),
        cost_estimate=pl.CostEstimate(flops=flops, bytes_accessed=nbytes, transcendentals=0),
    )(*operands)


def norm_kernel(tok_hbm, gain_hbm, down_hbm, up_hbm, last_hbm, normed_ref, down_ref, up_ref, last_ref,
                tok_ref, gain_ref, sem):
    pairs = ((tok_hbm, tok_ref), (gain_hbm, gain_ref), (down_hbm, down_ref), (up_hbm, up_ref),
             (last_hbm, last_ref))
    copies = [pltpu.make_async_copy(src, dst, sem.at[i]) for i, (src, dst) in enumerate(pairs)]
    for copy in copies:
        copy.start()
    for copy in copies[:2]:
        copy.wait()
    values = tok_ref[...].astype(F32)
    scale = lax.rsqrt(jnp.mean(values * values, axis=-1, keepdims=True) + epsilon)
    normed_ref[...] = (values * scale * gain_ref[...]).astype(BF16)
    for copy in copies[2:]:
        copy.wait()


def gate_kernel(top, normed_ref, list_hbm, router_hbm, ids_hbm, slot_hbm, wt_ref, list_ref, router_ref, ids_ref, slot_ref, sem):
    pairs = ((router_hbm, router_ref), (ids_hbm, ids_ref), (slot_hbm, slot_ref), (list_hbm, list_ref))
    copies = [pltpu.make_async_copy(src, dst, sem.at[i]) for i, (src, dst) in enumerate(pairs)]
    for copy in copies:
        copy.start()
    for copy in copies:
        copy.wait()
    logits = lax.dot_general(router_ref[...], normed_ref[...], (((1,), (1,)), ((), ())),
                             preferred_element_type=F32)
    sig = jax.nn.sigmoid(logits)
    experts, rows = sig.shape
    sub = lax.broadcasted_iota(jnp.int32, (experts, rows), 0)
    lane = lax.broadcasted_iota(jnp.int32, (experts, rows), 1)
    total = jnp.zeros((experts, rows), F32)
    served = jnp.zeros((experts, rows), F32)
    for k in range(top):
        hit = sub == ids_ref[k:k + 1, :]
        total = total + jnp.where(hit, 1.0, 0.0)
        served = served + jnp.where(hit & (slot_ref[k:k + 1, :] >= 0), 1.0, 0.0)
    _, shards, copies_n, local = list_ref.shape

    def listed(i, served):
        shard, copy = i // copies_n, i % copies_n
        for m in range(local):
            entry = list_ref[0, shard, copy, m]
            owner = jnp.where(entry >= 0, entry, -top) // top
            served = served + jnp.where((lane == owner) & (sub == shard * local + m), 1.0, 0.0)
        return served

    served = lax.fori_loop(0, shards * copies_n, listed, served)
    denom = jnp.sum(total * sig, axis=0, keepdims=True)
    wt_ref[...] = jnp.where(served > 0.0, sig / denom, 0.0)


def pile_kernel(*refs):
    depth = refs[0].shape[0]
    for i, x_ref in enumerate(refs[:-1]):
        refs[-1][i * depth:(i + 1) * depth, :] = x_ref[...]


def pick(chunks, other, depth, copies, normed_ref, x_ref):
    core, half, rep, group = here(copies)
    for i, (a, b) in enumerate(chunks):
        b = {"A": 2 + group, "B": 3 - group}.get(b, b)
        at = ((2 * (half ^ a) + (core ^ other)) * copies + (rep ^ b)) * depth
        x_ref[:, i * depth:(i + 1) * depth] = normed_ref[:, pl.ds(pl.multiple_of(at, depth), depth)]


def early_kernel(chunks, depth, copies, normed_ref, w0_ref, w1_ref, out_ref, x_ref):
    pick(chunks, 0, depth, copies, normed_ref, x_ref.at[0])
    pick(chunks, 1, depth, copies, normed_ref, x_ref.at[1])
    out_ref[...] = (jnp.dot(x_ref[0], w0_ref[...], preferred_element_type=F32)
                    + jnp.dot(x_ref[1], w1_ref[...], preferred_element_type=F32))


def late_kernel(chunks, copies, normed_ref, sum_ref, wt_ref, *refs):
    w_refs, (out_ref, x_ref, w_ref) = refs[:-3], refs[-3:]
    n = len(chunks)
    rows = normed_ref.shape[0]
    depth = w_refs[0].shape[0]
    for c in range(2):
        pick(chunks, c, depth, copies, normed_ref, x_ref.at[:, c * n * depth:(c + 1) * n * depth])
    for i, chunk in enumerate(w_refs):
        w_ref[i * depth:(i + 1) * depth, :] = chunk[...]
    out_ref[:rows, :] = (sum_ref[...] + jnp.dot(x_ref[...], w_ref[...],
                                                preferred_element_type=F32)).astype(BF16)
    wt = wt_ref[...]
    lead = wt.astype(BF16)
    out_ref[rows:, :rows] = lead
    out_ref[rows:, rows:] = (wt - lead.astype(F32)).astype(BF16)


def expert(x, weight, gate_w, up_w, down_w):
    gate = jnp.dot(x, gate_w, preferred_element_type=F32)
    upper = jnp.dot(x, up_w, preferred_element_type=F32)
    half = 0.5 * gate
    hidden = ((half + half * jnp.tanh(half)) * upper).astype(BF16)
    result = jnp.dot(hidden, down_w, preferred_element_type=F32).astype(BF16)
    return result.astype(F32) * weight


def columns(me, local, pay_ref, at, size):
    rows = pay_ref.shape[1] // 2
    wt = (pay_ref[rows:, at:at + size].astype(F32)
          + pay_ref[rows:, rows + at:rows + at + size].astype(F32))
    sub = lax.broadcasted_iota(jnp.int32, wt.shape, 0)
    picked = [jnp.sum(jnp.where(sub == (me ^ c) * local + j, wt, 0.0), axis=0, keepdims=True)
              for c in range(2) for j in range(local)]
    pad = [jnp.zeros((-len(picked) % 8, size), F32)] if len(picked) % 8 else []
    return jnp.concatenate(picked + pad, axis=0).T


def run_experts(span, at, size, pay_ref, w_refs, out_ref, start_ref=None):
    local = w_refs[0].shape[0]
    cols = columns(lax.axis_index("expert"), local, pay_ref, at, size)
    x = pay_ref[at:at + size, :]
    for j in span:
        refs = w_refs[:3] if j < local else w_refs[-3:]
        part = expert(x, cols[:, j:j + 1], *(ref[j % local] for ref in refs))
        if j == span[0]:
            out_ref[...] = part if start_ref is None else start_ref[at:at + size, :] + part
        else:
            out_ref[...] += part


def near_kernel(span, pay_ref, *refs):
    run_experts(span, 0, refs[-1].shape[0], pay_ref, refs[:-1], refs[-1])


def more_kernel(span, pay_ref, sum_ref, *refs):
    run_experts(span, 0, refs[-1].shape[0], pay_ref, refs[:-1], refs[-1], sum_ref)


def far_kernel(span, at, pay_ref, sum_ref, *refs):
    out_ref, acc_ref = refs[-2:]
    run_experts(span, at, out_ref.shape[0], pay_ref, refs[:6], acc_ref, sum_ref)
    out_ref[...] = acc_ref[...].astype(BF16)


def join_kernel(*refs):
    depth = refs[0].shape[0]
    for i, x_ref in enumerate(refs[:-1]):
        refs[-1][:, i * depth:(i + 1) * depth] = x_ref[...].T


def final_kernel(n_back, at, chunks, copies, depth, near_ref, *refs):
    out_ref, rows_ref, sem = refs[-3:]
    core, half, rep, group = here(copies)
    size = rows_ref.shape[0]
    total = near_ref[at:at + size, :]
    for s_ref in refs[:n_back]:
        total = total + s_ref[...].astype(F32)
    merged = total.astype(BF16)
    for (c, b), w_ref in zip(chunks, refs[n_back:]):
        b = {"A": 2 + group, "B": 3 - group}.get(b, b)
        block = jnp.dot(merged, w_ref[...], preferred_element_type=F32).astype(BF16)
        for a in range(w_ref.shape[1] // depth):
            e = 2 * (half ^ a) + (core ^ c)
            to = pl.multiple_of((e * copies + (rep ^ b)) * depth, depth)
            rows_ref[:, pl.ds(to, depth)] = block[:, a * depth:(a + 1) * depth]
    out = pltpu.make_async_copy(rows_ref, out_ref.at[pl.ds(at, size), :], sem)
    out.start()
    out.wait()


def shape(dims, dtype=BF16):
    return jax.ShapeDtypeStruct(dims, dtype)


def on_device(tokens, norm_gain, router, down_proj, up_proj, expert_gate, expert_up, expert_down,
              expert_ids, slot_pos, overflow_list):
    rows, width = tokens.shape
    top = expert_ids.shape[1]
    local, _, ff = expert_gate.shape
    depth, latent = down_proj.shape
    groups = lax.axis_size("groups")
    shards = lax.axis_size("expert")
    copies = lax.axis_size("replica")
    chips = shards // 2
    wide = copies * depth
    spread = copies
    if depth % 128:
        down_proj = lax.all_gather(down_proj, "replica", axis=0, tiled=True)
        up_proj = lax.all_gather(up_proj, "replica", axis=0, tiled=True)
        depth, spread = wide, 1
    experts = shards * local
    down = {(0, 0): down_proj}
    far_z = None
    if spread == groups + 2 and groups == 2:
        near_z = swap(down_proj, "replica", 1)
        far_z = swap_pair(down_proj, ("groups", "replica"), lambda i, j: (i, j ^ (2 + i)))
        down[(0, 1)] = near_z
        down[(0, "A")] = far_z
        for a in range(1, chips):
            down[(a, 0)] = swap(down_proj, "expert", 2 * a)
        ups_x = [swap(up_proj, "expert", 2 * a) for a in range(1, chips)]
        for a in range(1, chips):
            down[(a, 1)] = swap(near_z, "expert", 2 * a)
            down[(a, "B")] = swap_pair(far_z, ("groups", "expert"),
                                       lambda i, j: (i ^ 1, j ^ (2 * a)))
            down[(a, "A")] = swap(far_z, "expert", 2 * a)
        down[(0, "B")] = swap(far_z, "groups", 1)
    else:
        for b in range(1, spread):
            down[(0, b)] = swap(down_proj, "replica", b)
        for b in range(spread):
            for a in range(1, chips):
                down[(a, b)] = swap(down[(0, b)], "expert", 2 * a)
        ups_x = [swap(up_proj, "expert", 2 * a) for a in range(1, chips)]

    normed, own_down, own_up, last = kernel(
        norm_kernel, tuple(map(shape, ((rows, width), down_proj.shape, up_proj.shape,
                                       expert_down.shape))),
        tuple(map(in_hbm, (tokens, norm_gain.reshape(1, width), down_proj, up_proj, expert_down))),
        [AN] * 5, 18, 8 * rows * width, 4 * rows * width,
        [pltpu.VMEM((rows, width), BF16), pltpu.VMEM((1, width), F32), pltpu.SemaphoreType.DMA((5,))])
    wt = kernel(
        functools.partial(gate_kernel, top), shape((experts, rows), F32),
        (normed, *map(in_hbm, (overflow_list, router.T, expert_ids.T, slot_pos.T))),
        [VM] + [AN] * 4, 10, 4 * rows * width * experts, 2 * rows * width,
        [pltpu.SMEM(overflow_list.shape, jnp.int32), pltpu.VMEM((experts, width), BF16),
         pltpu.VMEM((top, rows), jnp.int32), pltpu.VMEM((top, rows), jnp.int32),
         pltpu.SemaphoreType.DMA((4,))])
    down[(0, 0)] = own_down
    weights = (expert_gate, expert_up, last, *[
        swap(w, "expert", 1) for w in (expert_gate, expert_up, expert_down)])

    late = [k for k in down if (k[1] == "A" and k[0]) or k[1] == "B"] or list(down)[-1:]
    early = [k for k in down if k not in late]

    n = len(early)
    stacked = kernel(pile_kernel, shape((n * depth, latent)), [down[k] for k in early], [VM] * n,
                     6, 0, 4 * n * depth * latent)
    stacked_core = swap(stacked, "expert", 1)
    late_core = [swap(down[k], "expert", 1) for k in late]
    opened = kernel(
        functools.partial(early_kernel, early, depth, spread), shape((rows, latent), F32),
        (normed, stacked, stacked_core), [VM] * 3, 10, 4 * rows * n * depth * latent,
        4 * n * depth * latent, [pltpu.VMEM((2, rows, n * depth), BF16)])
    n = len(late)
    own = kernel(
        functools.partial(late_kernel, late, spread), shape((rows + experts, latent)),
        (normed, opened, wt, *[down[k] for k in late], *late_core), [VM] * (3 + 2 * n), 10,
        4 * rows * n * depth * latent, 4 * n * depth * latent,
        [pltpu.VMEM((rows, 2 * n * depth), BF16), pltpu.VMEM((2 * n * depth, latent), BF16)])
    work = 6 * rows * latent * ff
    load = 6 * latent * ff
    count = 2 * local
    cut = count - local // 2
    far = [swap(own, "expert", 2 * a) for a in range(1, chips)]

    def run(body, operands, span):
        return kernel(
            functools.partial(body, span), shape((rows, latent), F32), operands, [VM] * len(operands),
            16, len(span) * work, len(span) * load)

    near = run(near_kernel, (own, *weights[:3]), range(local))
    near = run(more_kernel, (own, near, *weights), range(local, cut))
    near = run(more_kernel, (own, near, *weights), range(cut, count))
    parts = 2
    size = rows // parts
    back = [[] for _ in range(parts)]
    for a in range(1, chips):
        opened = run(near_kernel, (far[a - 1], *weights), range(cut))
        for h in range(parts):
            s = kernel(
                functools.partial(far_kernel, range(cut, count), h * size),
                shape((size, latent)), (far[a - 1], opened, *weights), [VM] * 8, 14,
                (count - cut) * work // parts, (count - cut) * load, [pltpu.VMEM((size, latent), F32)])
            back[h].append(swap(s, "expert", 2 * a))

    pair = kernel(join_kernel, shape((latent, chips * depth)), (own_up, *ups_x),
                  [VM] * chips, 4, 0, 4 * chips * depth * latent)
    ups = {(0, 0): pair}
    if far_z is not None:
        ups[(0, 1)] = swap(pair, "replica", 1)
        ups[(0, "A")] = swap_pair(pair, ("groups", "replica"), lambda i, j: (i, j ^ (2 + i)))
        ups[(0, "B")] = swap(ups[(0, "A")], "groups", 1)
    else:
        for b in range(1, spread):
            ups[(0, b)] = swap(pair, "replica", b)
    for _, b in list(ups):
        ups[(1, b)] = swap(ups[(0, b)], "expert", 1)
    order = list(ups)
    result = None
    for h in range(parts):
        operands = (near, *back[h], *[ups[k] for k in order])
        result = kernel(
            functools.partial(final_kernel, len(back[h]), h * size, order, spread, depth),
            shape((rows, width)), operands + ((result,) if h else ()),
            [VM] * len(operands) + [AN] * h, 10, 2 * size * width * latent, 2 * width * latent,
            [pltpu.VMEM((size, width), BF16), pltpu.SemaphoreType.DMA],
            AN, {len(operands): 0} if h else {})
    return result


def solution(mesh):
    placed = (
        P(("groups", "expert", "replica"), None),
        P(),
        P(),
        P(("expert", "replica"), None),
        P(("expert", "replica"), None),
        P("expert", None, None),
        P("expert", None, None),
        P("expert", None, None),
        P(("groups", "expert", "replica"), None),
        P(("groups", "expert", "replica"), None),
        P(("groups", "expert", "replica"), None, None, None),
    )

    return jax.shard_map(
        on_device,
        mesh=mesh,
        in_specs=placed,
        out_specs=P(("groups", "expert", "replica"), None),
        check_vma=False,
    )
```

```python
import functools

import jax
import jax.numpy as jnp
from jax import lax
from jax.experimental import pallas as pl
from jax.experimental.pallas import tpu as pltpu
from jax.sharding import PartitionSpec as P

epsilon = 1e-06
F32 = jnp.float32
BF16 = jnp.bfloat16

VM = pl.BlockSpec(memory_space=pltpu.VMEM)
AN = pl.BlockSpec(memory_space=pl.ANY)


def here(copies):
    e = lax.axis_index("expert")
    rep = lax.axis_index("replica") if copies > 1 else 0
    return lax.rem(e, 2), e // 2, rep, lax.axis_index("groups")


def in_hbm(x):
    return pltpu.with_memory_space_constraint(x, pltpu.HBM)


def swap(x, axis, bits):
    size = lax.axis_size(axis)
    return lax.ppermute(x, axis, [(i, i ^ bits) for i in range(size)])


def swap_pair(x, axes, move):
    sizes = [lax.axis_size(axis) for axis in axes]
    pairs = []
    for i in range(sizes[0]):
        for j in range(sizes[1]):
            p, q = move(i, j)
            pairs.append((i * sizes[1] + j, p * sizes[1] + q))
    return lax.ppermute(x, axes, pairs)


def kernel(body, out_shape, operands, specs, mib, flops=0, nbytes=0, scratch=(), out_specs=None,
           aliases={}):
    many = isinstance(out_shape, tuple)
    if out_specs is None:
        out_specs = (VM,) * len(out_shape) if many else VM
    return pl.pallas_call(
        body,
        out_shape=out_shape,
        in_specs=specs,
        out_specs=out_specs,
        scratch_shapes=list(scratch),
        input_output_aliases=aliases,
        compiler_params=pltpu.CompilerParams(vmem_limit_bytes=mib * 1024 * 1024),
        cost_estimate=pl.CostEstimate(flops=flops, bytes_accessed=nbytes, transcendentals=0),
    )(*operands)


def norm_kernel(tok_hbm, gain_hbm, *refs):
    n = (len(refs) - 4) // 2
    normed_ref, (tok_ref, gain_ref, sem) = refs[n], refs[-3:]
    pairs = ((tok_hbm, tok_ref), (gain_hbm, gain_ref), *zip(refs[:n], refs[n + 1:-3]))
    copies = [pltpu.make_async_copy(src, dst, sem.at[i]) for i, (src, dst) in enumerate(pairs)]
    for copy in copies:
        copy.start()
    for copy in copies[:2]:
        copy.wait()
    values = tok_ref[...].astype(F32)
    scale = lax.rsqrt(jnp.mean(values * values, axis=-1, keepdims=True) + epsilon)
    normed_ref[...] = (values * scale * gain_ref[...]).astype(BF16)
    for copy in copies[2:]:
        copy.wait()


def gate_kernel(top, normed_ref, router_ref, ids_ref, slot_ref, list_hbm, wt_ref, list_ref, sem):
    load = pltpu.make_async_copy(list_hbm, list_ref, sem)
    load.start()
    logits = lax.dot_general(router_ref[...], normed_ref[...], (((1,), (1,)), ((), ())),
                             preferred_element_type=F32)
    sig = jax.nn.sigmoid(logits)
    experts, rows = sig.shape
    sub = lax.broadcasted_iota(jnp.int32, (experts, rows), 0)
    lane = lax.broadcasted_iota(jnp.int32, (experts, rows), 1)
    total = jnp.zeros((experts, rows), F32)
    served = jnp.zeros((experts, rows), F32)
    for k in range(top):
        hit = sub == ids_ref[k:k + 1, :]
        total = total + jnp.where(hit, 1.0, 0.0)
        served = served + jnp.where(hit & (slot_ref[k:k + 1, :] >= 0), 1.0, 0.0)
    load.wait()
    _, shards, copies_n, local = list_ref.shape

    def listed(i, served):
        shard, copy = i // copies_n, i % copies_n
        for m in range(local):
            entry = list_ref[0, shard, copy, m]
            owner = jnp.where(entry >= 0, entry, -top) // top
            served = served + jnp.where((lane == owner) & (sub == shard * local + m), 1.0, 0.0)
        return served

    served = lax.fori_loop(0, shards * copies_n, listed, served)
    denom = jnp.sum(total * sig, axis=0, keepdims=True)
    wt_ref[...] = jnp.where(served > 0.0, sig / denom, 0.0)


def pile_kernel(*refs):
    depth = refs[0].shape[0]
    for i, x_ref in enumerate(refs[:-1]):
        refs[-1][i * depth:(i + 1) * depth, :] = x_ref[...]


def pick(chunks, other, depth, copies, normed_ref, x_ref):
    core, half, rep, group = here(copies)
    for i, (a, b) in enumerate(chunks):
        b = {"A": 2 + group, "B": 3 - group}.get(b, b)
        at = ((2 * (half ^ a) + (core ^ other)) * copies + (rep ^ b)) * depth
        x_ref[:, i * depth:(i + 1) * depth] = normed_ref[:, pl.ds(pl.multiple_of(at, depth), depth)]


def early_kernel(chunks, depth, copies, normed_ref, w0_ref, w1_ref, out_ref, x_ref):
    pick(chunks, 0, depth, copies, normed_ref, x_ref.at[0])
    pick(chunks, 1, depth, copies, normed_ref, x_ref.at[1])
    out_ref[...] = (jnp.dot(x_ref[0], w0_ref[...], preferred_element_type=F32)
                    + jnp.dot(x_ref[1], w1_ref[...], preferred_element_type=F32))


def late_kernel(chunks, copies, normed_ref, sum_ref, wt_ref, *refs):
    w_refs, (out_ref, x_ref, w_ref) = refs[:-3], refs[-3:]
    n = len(chunks)
    rows = normed_ref.shape[0]
    depth = w_refs[0].shape[0]
    for c in range(2):
        pick(chunks, c, depth, copies, normed_ref, x_ref.at[:, c * n * depth:(c + 1) * n * depth])
    for i, chunk in enumerate(w_refs):
        w_ref[i * depth:(i + 1) * depth, :] = chunk[...]
    out_ref[:rows, :] = (sum_ref[...] + jnp.dot(x_ref[...], w_ref[...],
                                                preferred_element_type=F32)).astype(BF16)
    wt = wt_ref[...]
    lead = wt.astype(BF16)
    out_ref[rows:, :rows] = lead
    out_ref[rows:, rows:] = (wt - lead.astype(F32)).astype(BF16)


def expert(x, weight, gate_w, up_w, down_w):
    gate = jnp.dot(x, gate_w, preferred_element_type=F32)
    upper = jnp.dot(x, up_w, preferred_element_type=F32)
    half = 0.5 * gate
    hidden = ((half + half * jnp.tanh(half)) * upper).astype(BF16)
    result = jnp.dot(hidden, down_w, preferred_element_type=F32).astype(BF16)
    return result.astype(F32) * weight


def columns(me, local, pay_ref, at, size):
    rows = pay_ref.shape[1] // 2
    wt = (pay_ref[rows:, at:at + size].astype(F32)
          + pay_ref[rows:, rows + at:rows + at + size].astype(F32))
    sub = lax.broadcasted_iota(jnp.int32, wt.shape, 0)
    picked = [jnp.sum(jnp.where(sub == (me ^ c) * local + j, wt, 0.0), axis=0, keepdims=True)
              for c in range(2) for j in range(local)]
    pad = [jnp.zeros((-len(picked) % 8, size), F32)] if len(picked) % 8 else []
    return jnp.concatenate(picked + pad, axis=0).T


def run_experts(span, at, size, pay_ref, w_refs, out_ref, start_ref=None):
    local = w_refs[0].shape[0]
    cols = columns(lax.axis_index("expert"), local, pay_ref, at, size)
    x = pay_ref[at:at + size, :]
    for j in span:
        refs = w_refs[:3] if j < local else w_refs[-3:]
        part = expert(x, cols[:, j:j + 1], *(ref[j % local] for ref in refs))
        if j == span[0]:
            out_ref[...] = part if start_ref is None else start_ref[at:at + size, :] + part
        else:
            out_ref[...] += part


def near_kernel(span, pay_ref, *refs):
    run_experts(span, 0, refs[-1].shape[0], pay_ref, refs[:-1], refs[-1])


def more_kernel(span, pay_ref, sum_ref, *refs):
    run_experts(span, 0, refs[-1].shape[0], pay_ref, refs[:-1], refs[-1], sum_ref)


def far_kernel(span, at, pay_ref, sum_ref, *refs):
    out_ref, acc_ref = refs[-2:]
    run_experts(span, at, out_ref.shape[0], pay_ref, refs[:6], acc_ref, sum_ref)
    out_ref[...] = acc_ref[...].astype(BF16)


def join_kernel(*refs):
    depth = refs[0].shape[0]
    for i, x_ref in enumerate(refs[:-1]):
        refs[-1][:, i * depth:(i + 1) * depth] = x_ref[...].T


def final_kernel(n_back, at, chunks, copies, depth, near_ref, *refs):
    out_ref, rows_ref, sem = refs[-3:]
    core, half, rep, group = here(copies)
    size = rows_ref.shape[0]
    total = near_ref[at:at + size, :]
    for s_ref in refs[:n_back]:
        total = total + s_ref[...].astype(F32)
    merged = total.astype(BF16)
    for (c, b), w_ref in zip(chunks, refs[n_back:]):
        b = {"A": 2 + group, "B": 3 - group}.get(b, b)
        block = jnp.dot(merged, w_ref[...], preferred_element_type=F32).astype(BF16)
        for a in range(w_ref.shape[1] // depth):
            e = 2 * (half ^ a) + (core ^ c)
            to = pl.multiple_of((e * copies + (rep ^ b)) * depth, depth)
            rows_ref[:, pl.ds(to, depth)] = block[:, a * depth:(a + 1) * depth]
    out = pltpu.make_async_copy(rows_ref, out_ref.at[pl.ds(at, size), :], sem)
    out.start()
    out.wait()


def shape(dims, dtype=BF16):
    return jax.ShapeDtypeStruct(dims, dtype)


def on_device(tokens, norm_gain, router, down_proj, up_proj, expert_gate, expert_up, expert_down,
              expert_ids, slot_pos, overflow_list):
    rows, width = tokens.shape
    top = expert_ids.shape[1]
    local, _, ff = expert_gate.shape
    depth, latent = down_proj.shape
    groups = lax.axis_size("groups")
    shards = lax.axis_size("expert")
    copies = lax.axis_size("replica")
    chips = shards // 2
    wide = copies * depth
    spread = copies
    if depth % 128:
        down_proj = lax.all_gather(down_proj, "replica", axis=0, tiled=True)
        up_proj = lax.all_gather(up_proj, "replica", axis=0, tiled=True)
        depth, spread = wide, 1
    experts = shards * local
    down = {(0, 0): down_proj}
    far_z = None
    if spread == groups + 2 and groups == 2:
        near_z = swap(down_proj, "replica", 1)
        far_z = swap_pair(down_proj, ("groups", "replica"), lambda i, j: (i, j ^ (2 + i)))
        down[(0, 1)] = near_z
        down[(0, "A")] = far_z
        for a in range(1, chips):
            down[(a, 0)] = swap(down_proj, "expert", 2 * a)
        ups_x = [swap(up_proj, "expert", 2 * a) for a in range(1, chips)]
        for a in range(1, chips):
            down[(a, 1)] = swap(near_z, "expert", 2 * a)
            down[(a, "B")] = swap_pair(far_z, ("groups", "expert"),
                                       lambda i, j: (i ^ 1, j ^ (2 * a)))
            down[(a, "A")] = swap(far_z, "expert", 2 * a)
        down[(0, "B")] = swap(far_z, "groups", 1)
    else:
        for b in range(1, spread):
            down[(0, b)] = swap(down_proj, "replica", b)
        for b in range(spread):
            for a in range(1, chips):
                down[(a, b)] = swap(down[(0, b)], "expert", 2 * a)
        ups_x = [swap(up_proj, "expert", 2 * a) for a in range(1, chips)]

    moved = (down_proj, up_proj, expert_down, router.T, expert_ids.T, slot_pos.T)
    normed, own_down, own_up, last, *routing = kernel(
        norm_kernel, (shape((rows, width)), *[shape(x.shape, x.dtype) for x in moved]),
        tuple(map(in_hbm, (tokens, norm_gain.reshape(1, width), *moved))), [AN] * (2 + len(moved)), 18,
        8 * rows * width, 4 * rows * width,
        [pltpu.VMEM((rows, width), BF16), pltpu.VMEM((1, width), F32),
         pltpu.SemaphoreType.DMA((2 + len(moved),))])
    wt = kernel(
        functools.partial(gate_kernel, top), shape((experts, rows), F32),
        (normed, *routing, in_hbm(overflow_list)), [VM] * 4 + [AN], 10, 4 * rows * width * experts,
        2 * rows * width, [pltpu.SMEM(overflow_list.shape, jnp.int32), pltpu.SemaphoreType.DMA])
    down[(0, 0)] = own_down
    weights = (expert_gate, expert_up, last, *[
        swap(w, "expert", 1) for w in (expert_gate, expert_up, expert_down)])

    late = [k for k in down if (k[1] == "A" and k[0]) or k[1] == "B"] or list(down)[-1:]
    early = [k for k in down if k not in late]

    n = len(early)
    stacked = kernel(pile_kernel, shape((n * depth, latent)), [down[k] for k in early], [VM] * n,
                     6, 0, 4 * n * depth * latent)
    stacked_core = swap(stacked, "expert", 1)
    late_core = [swap(down[k], "expert", 1) for k in late]
    opened = kernel(
        functools.partial(early_kernel, early, depth, spread), shape((rows, latent), F32),
        (normed, stacked, stacked_core), [VM] * 3, 10, 4 * rows * n * depth * latent,
        4 * n * depth * latent, [pltpu.VMEM((2, rows, n * depth), BF16)])
    n = len(late)
    own = kernel(
        functools.partial(late_kernel, late, spread), shape((rows + experts, latent)),
        (normed, opened, wt, *[down[k] for k in late], *late_core), [VM] * (3 + 2 * n), 10,
        4 * rows * n * depth * latent, 4 * n * depth * latent,
        [pltpu.VMEM((rows, 2 * n * depth), BF16), pltpu.VMEM((2 * n * depth, latent), BF16)])
    work = 6 * rows * latent * ff
    load = 6 * latent * ff
    count = 2 * local
    cut = count - local // 2
    far = [swap(own, "expert", 2 * a) for a in range(1, chips)]

    def run(body, operands, span):
        return kernel(
            functools.partial(body, span), shape((rows, latent), F32), operands, [VM] * len(operands),
            16, len(span) * work, len(span) * load)

    near = run(near_kernel, (own, *weights[:3]), range(local))
    near = run(more_kernel, (own, near, *weights), range(local, cut))
    near = run(more_kernel, (own, near, *weights), range(cut, count))
    parts = 2
    size = rows // parts
    back = [[] for _ in range(parts)]
    for a in range(1, chips):
        opened = run(near_kernel, (far[a - 1], *weights[:3]), range(local))
        opened = run(more_kernel, (far[a - 1], opened, *weights), range(local, cut))
        for h in range(parts):
            s = kernel(
                functools.partial(far_kernel, range(cut, count), h * size),
                shape((size, latent)), (far[a - 1], opened, *weights), [VM] * 8, 14,
                (count - cut) * work // parts, (count - cut) * load, [pltpu.VMEM((size, latent), F32)])
            back[h].append(swap(s, "expert", 2 * a))

    pair = kernel(join_kernel, shape((latent, chips * depth)), (own_up, *ups_x),
                  [VM] * chips, 4, 0, 4 * chips * depth * latent)
    ups = {(0, 0): pair}
    if far_z is not None:
        ups[(0, 1)] = swap(pair, "replica", 1)
        ups[(0, "A")] = swap_pair(pair, ("groups", "replica"), lambda i, j: (i, j ^ (2 + i)))
        ups[(0, "B")] = swap(ups[(0, "A")], "groups", 1)
    else:
        for b in range(1, spread):
            ups[(0, b)] = swap(pair, "replica", b)
    for _, b in list(ups):
        ups[(1, b)] = swap(ups[(0, b)], "expert", 1)
    order = list(ups)
    result = None
    for h in range(parts):
        operands = (near, *back[h], *[ups[k] for k in order])
        result = kernel(
            functools.partial(final_kernel, len(back[h]), h * size, order, spread, depth),
            shape((rows, width)), operands + ((result,) if h else ()),
            [VM] * len(operands) + [AN] * h, 10, 2 * size * width * latent, 2 * width * latent,
            [pltpu.VMEM((size, width), BF16), pltpu.SemaphoreType.DMA],
            AN, {len(operands): 0} if h else {})
    return result


def solution(mesh):
    placed = (
        P(("groups", "expert", "replica"), None),
        P(),
        P(),
        P(("expert", "replica"), None),
        P(("expert", "replica"), None),
        P("expert", None, None),
        P("expert", None, None),
        P("expert", None, None),
        P(("groups", "expert", "replica"), None),
        P(("groups", "expert", "replica"), None),
        P(("groups", "expert", "replica"), None, None, None),
    )

    return jax.shard_map(
        on_device,
        mesh=mesh,
        in_specs=placed,
        out_specs=P(("groups", "expert", "replica"), None),
        check_vma=False,
    )
```

```python
import functools

import jax
import jax.numpy as jnp
from jax import lax
from jax.experimental import pallas as pl
from jax.experimental.pallas import tpu as pltpu
from jax.sharding import PartitionSpec as P

epsilon = 1e-06
F32 = jnp.float32
BF16 = jnp.bfloat16

VM = pl.BlockSpec(memory_space=pltpu.VMEM)
AN = pl.BlockSpec(memory_space=pl.ANY)


def here(copies):
    e = lax.axis_index("expert")
    rep = lax.axis_index("replica") if copies > 1 else 0
    return lax.rem(e, 2), e // 2, rep, lax.axis_index("groups")


def in_hbm(x):
    return pltpu.with_memory_space_constraint(x, pltpu.HBM)


def swap(x, axis, bits):
    size = lax.axis_size(axis)
    return lax.ppermute(x, axis, [(i, i ^ bits) for i in range(size)])


def swap_pair(x, axes, move):
    sizes = [lax.axis_size(axis) for axis in axes]
    pairs = []
    for i in range(sizes[0]):
        for j in range(sizes[1]):
            p, q = move(i, j)
            pairs.append((i * sizes[1] + j, p * sizes[1] + q))
    return lax.ppermute(x, axes, pairs)


def kernel(body, out_shape, operands, specs, mib, flops=0, nbytes=0, scratch=(), out_specs=None,
           aliases={}):
    many = isinstance(out_shape, tuple)
    if out_specs is None:
        out_specs = (VM,) * len(out_shape) if many else VM
    return pl.pallas_call(
        body,
        out_shape=out_shape,
        in_specs=specs,
        out_specs=out_specs,
        scratch_shapes=list(scratch),
        input_output_aliases=aliases,
        compiler_params=pltpu.CompilerParams(vmem_limit_bytes=mib * 1024 * 1024),
        cost_estimate=pl.CostEstimate(flops=flops, bytes_accessed=nbytes, transcendentals=0),
    )(*operands)


def norm_kernel(tok_hbm, gain_hbm, *refs):
    n = (len(refs) - 4) // 2
    normed_ref, (tok_ref, gain_ref, sem) = refs[n], refs[-3:]
    pairs = ((tok_hbm, tok_ref), (gain_hbm, gain_ref), *zip(refs[:n], refs[n + 1:-3]))
    copies = [pltpu.make_async_copy(src, dst, sem.at[i]) for i, (src, dst) in enumerate(pairs)]
    for copy in copies:
        copy.start()
    for copy in copies[:2]:
        copy.wait()
    values = tok_ref[...].astype(F32)
    scale = lax.rsqrt(jnp.mean(values * values, axis=-1, keepdims=True) + epsilon)
    normed_ref[...] = (values * scale * gain_ref[...]).astype(BF16)
    for copy in copies[2:]:
        copy.wait()


def gate_kernel(top, normed_ref, router_ref, ids_ref, slot_ref, list_hbm, wt_ref, list_ref, sem):
    load = pltpu.make_async_copy(list_hbm, list_ref, sem)
    load.start()
    logits = lax.dot_general(router_ref[...], normed_ref[...], (((1,), (1,)), ((), ())),
                             preferred_element_type=F32)
    sig = jax.nn.sigmoid(logits)
    experts, rows = sig.shape
    sub = lax.broadcasted_iota(jnp.int32, (experts, rows), 0)
    lane = lax.broadcasted_iota(jnp.int32, (experts, rows), 1)
    total = jnp.zeros((experts, rows), F32)
    served = jnp.zeros((experts, rows), F32)
    for k in range(top):
        hit = sub == ids_ref[k:k + 1, :]
        total = total + jnp.where(hit, 1.0, 0.0)
        served = served + jnp.where(hit & (slot_ref[k:k + 1, :] >= 0), 1.0, 0.0)
    load.wait()
    _, shards, copies_n, local = list_ref.shape

    def listed(i, served):
        shard, copy = i // copies_n, i % copies_n
        for m in range(local):
            entry = list_ref[0, shard, copy, m]
            owner = jnp.where(entry >= 0, entry, -top) // top
            served = served + jnp.where((lane == owner) & (sub == shard * local + m), 1.0, 0.0)
        return served

    served = lax.fori_loop(0, shards * copies_n, listed, served)
    denom = jnp.sum(total * sig, axis=0, keepdims=True)
    wt_ref[...] = jnp.where(served > 0.0, sig / denom, 0.0)


def pile_kernel(*refs):
    depth = refs[0].shape[0]
    for i, x_ref in enumerate(refs[:-1]):
        refs[-1][i * depth:(i + 1) * depth, :] = x_ref[...]


def pick(chunks, other, depth, copies, normed_ref, x_ref):
    core, half, rep, group = here(copies)
    for i, (a, b) in enumerate(chunks):
        b = {"A": 2 + group, "B": 3 - group}.get(b, b)
        at = ((2 * (half ^ a) + (core ^ other)) * copies + (rep ^ b)) * depth
        x_ref[:, i * depth:(i + 1) * depth] = normed_ref[:, pl.ds(pl.multiple_of(at, depth), depth)]


def early_kernel(chunks, depth, copies, normed_ref, w0_ref, w1_ref, out_ref, x_ref):
    pick(chunks, 0, depth, copies, normed_ref, x_ref.at[0])
    pick(chunks, 1, depth, copies, normed_ref, x_ref.at[1])
    out_ref[...] = (jnp.dot(x_ref[0], w0_ref[...], preferred_element_type=F32)
                    + jnp.dot(x_ref[1], w1_ref[...], preferred_element_type=F32))


def late_kernel(chunks, copies, normed_ref, sum_ref, wt_ref, *refs):
    w_refs, (out_ref, x_ref, w_ref) = refs[:-3], refs[-3:]
    n = len(chunks)
    rows = normed_ref.shape[0]
    depth = w_refs[0].shape[0]
    for c in range(2):
        pick(chunks, c, depth, copies, normed_ref, x_ref.at[:, c * n * depth:(c + 1) * n * depth])
    for i, chunk in enumerate(w_refs):
        w_ref[i * depth:(i + 1) * depth, :] = chunk[...]
    out_ref[:rows, :] = (sum_ref[...] + jnp.dot(x_ref[...], w_ref[...],
                                                preferred_element_type=F32)).astype(BF16)
    wt = wt_ref[...]
    lead = wt.astype(BF16)
    out_ref[rows:, :rows] = lead
    out_ref[rows:, rows:] = (wt - lead.astype(F32)).astype(BF16)


def expert(x, weight, gate_w, up_w, down_w):
    gate = jnp.dot(x, gate_w, preferred_element_type=F32)
    upper = jnp.dot(x, up_w, preferred_element_type=F32)
    half = 0.5 * gate
    hidden = ((half + half * jnp.tanh(half)) * upper).astype(BF16)
    result = jnp.dot(hidden, down_w, preferred_element_type=F32).astype(BF16)
    return result.astype(F32) * weight


def columns(me, local, pay_ref, at, size):
    rows = pay_ref.shape[1] // 2
    wt = (pay_ref[rows:, at:at + size].astype(F32)
          + pay_ref[rows:, rows + at:rows + at + size].astype(F32))
    sub = lax.broadcasted_iota(jnp.int32, wt.shape, 0)
    picked = [jnp.sum(jnp.where(sub == (me ^ c) * local + j, wt, 0.0), axis=0, keepdims=True)
              for c in range(2) for j in range(local)]
    pad = [jnp.zeros((-len(picked) % 8, size), F32)] if len(picked) % 8 else []
    return jnp.concatenate(picked + pad, axis=0).T


def run_experts(span, at, size, pay_ref, w_refs, out_ref, start_ref=None):
    local = w_refs[0].shape[0]
    cols = columns(lax.axis_index("expert"), local, pay_ref, at, size)
    x = pay_ref[at:at + size, :]
    for j in span:
        refs = w_refs[:3] if j < local else w_refs[-3:]
        part = expert(x, cols[:, j:j + 1], *(ref[j % local] for ref in refs))
        if j == span[0]:
            out_ref[...] = part if start_ref is None else start_ref[at:at + size, :] + part
        else:
            out_ref[...] += part


def near_kernel(span, pay_ref, *refs):
    run_experts(span, 0, refs[-1].shape[0], pay_ref, refs[:-1], refs[-1])


def more_kernel(span, pay_ref, sum_ref, *refs):
    run_experts(span, 0, refs[-1].shape[0], pay_ref, refs[:-1], refs[-1], sum_ref)


def far_kernel(span, at, pay_ref, sum_ref, *refs):
    out_ref, acc_ref = refs[-2:]
    run_experts(span, at, out_ref.shape[0], pay_ref, refs[:6], acc_ref, sum_ref)
    out_ref[...] = acc_ref[...].astype(BF16)


def join_kernel(*refs):
    depth = refs[0].shape[0]
    for i, x_ref in enumerate(refs[:-1]):
        refs[-1][:, i * depth:(i + 1) * depth] = x_ref[...].T


def final_kernel(n_back, at, chunks, copies, depth, near_ref, *refs):
    out_ref, rows_ref, sem = refs[-3:]
    core, half, rep, group = here(copies)
    size = rows_ref.shape[0]
    total = near_ref[at:at + size, :]
    for s_ref in refs[:n_back]:
        total = total + s_ref[...].astype(F32)
    merged = total.astype(BF16)
    for (c, b), w_ref in zip(chunks, refs[n_back:]):
        b = {"A": 2 + group, "B": 3 - group}.get(b, b)
        block = jnp.dot(merged, w_ref[...], preferred_element_type=F32).astype(BF16)
        for a in range(w_ref.shape[1] // depth):
            e = 2 * (half ^ a) + (core ^ c)
            to = pl.multiple_of((e * copies + (rep ^ b)) * depth, depth)
            rows_ref[:, pl.ds(to, depth)] = block[:, a * depth:(a + 1) * depth]
    out = pltpu.make_async_copy(rows_ref, out_ref.at[pl.ds(at, size), :], sem)
    out.start()
    out.wait()


def shape(dims, dtype=BF16):
    return jax.ShapeDtypeStruct(dims, dtype)


def on_device(tokens, norm_gain, router, down_proj, up_proj, expert_gate, expert_up, expert_down,
              expert_ids, slot_pos, overflow_list):
    rows, width = tokens.shape
    top = expert_ids.shape[1]
    local, _, ff = expert_gate.shape
    depth, latent = down_proj.shape
    groups = lax.axis_size("groups")
    shards = lax.axis_size("expert")
    copies = lax.axis_size("replica")
    chips = shards // 2
    wide = copies * depth
    spread = copies
    if depth % 128:
        down_proj = lax.all_gather(down_proj, "replica", axis=0, tiled=True)
        up_proj = lax.all_gather(up_proj, "replica", axis=0, tiled=True)
        depth, spread = wide, 1
    experts = shards * local
    down = {(0, 0): down_proj}
    far_z = None
    if spread == groups + 2 and groups == 2:
        near_z = swap(down_proj, "replica", 1)
        far_z = swap_pair(down_proj, ("groups", "replica"), lambda i, j: (i, j ^ (2 + i)))
        down[(0, 1)] = near_z
        down[(0, "A")] = far_z
        for a in range(1, chips):
            down[(a, 0)] = swap(down_proj, "expert", 2 * a)
        ups_x = [swap(up_proj, "expert", 2 * a) for a in range(1, chips)]
        for a in range(1, chips):
            down[(a, 1)] = swap(near_z, "expert", 2 * a)
            down[(a, "B")] = swap_pair(far_z, ("groups", "expert"),
                                       lambda i, j: (i ^ 1, j ^ (2 * a)))
            down[(a, "A")] = swap(far_z, "expert", 2 * a)
        down[(0, "B")] = swap(far_z, "groups", 1)
    else:
        for b in range(1, spread):
            down[(0, b)] = swap(down_proj, "replica", b)
        for b in range(spread):
            for a in range(1, chips):
                down[(a, b)] = swap(down[(0, b)], "expert", 2 * a)
        ups_x = [swap(up_proj, "expert", 2 * a) for a in range(1, chips)]

    moved = (down_proj, up_proj, expert_down, router.T, expert_ids.T, slot_pos.T)
    normed, own_down, own_up, last, *routing = kernel(
        norm_kernel, (shape((rows, width)), *[shape(x.shape, x.dtype) for x in moved]),
        tuple(map(in_hbm, (tokens, norm_gain.reshape(1, width), *moved))), [AN] * (2 + len(moved)), 18,
        8 * rows * width, 4 * rows * width,
        [pltpu.VMEM((rows, width), BF16), pltpu.VMEM((1, width), F32),
         pltpu.SemaphoreType.DMA((2 + len(moved),))])
    wt = kernel(
        functools.partial(gate_kernel, top), shape((experts, rows), F32),
        (normed, *routing, in_hbm(overflow_list)), [VM] * 4 + [AN], 10, 4 * rows * width * experts,
        2 * rows * width, [pltpu.SMEM(overflow_list.shape, jnp.int32), pltpu.SemaphoreType.DMA])
    down[(0, 0)] = own_down
    weights = (expert_gate, expert_up, last, *[
        swap(w, "expert", 1) for w in (expert_gate, expert_up, expert_down)])

    late = [k for k in down if (k[1] == "A" and k[0]) or k[1] == "B"] or list(down)[-1:]
    early = [k for k in down if k not in late]

    n = len(early)
    stacked = kernel(pile_kernel, shape((n * depth, latent)), [down[k] for k in early], [VM] * n,
                     6, 0, 4 * n * depth * latent)
    stacked_core = swap(stacked, "expert", 1)
    late_core = [swap(down[k], "expert", 1) for k in late]
    opened = kernel(
        functools.partial(early_kernel, early, depth, spread), shape((rows, latent), F32),
        (normed, stacked, stacked_core), [VM] * 3, 10, 4 * rows * n * depth * latent,
        4 * n * depth * latent, [pltpu.VMEM((2, rows, n * depth), BF16)])
    n = len(late)
    own = kernel(
        functools.partial(late_kernel, late, spread), shape((rows + experts, latent)),
        (normed, opened, wt, *[down[k] for k in late], *late_core), [VM] * (3 + 2 * n), 10,
        4 * rows * n * depth * latent, 4 * n * depth * latent,
        [pltpu.VMEM((rows, 2 * n * depth), BF16), pltpu.VMEM((2 * n * depth, latent), BF16)])
    work = 6 * rows * latent * ff
    load = 6 * latent * ff
    count = 2 * local
    cut = count - local // 2
    far = [swap(own, "expert", 2 * a) for a in range(1, chips)]

    def run(body, operands, span):
        return kernel(
            functools.partial(body, span), shape((rows, latent), F32), operands, [VM] * len(operands),
            16, len(span) * work, len(span) * load)

    near = run(near_kernel, (own, *weights[:3]), range(local))
    near = run(more_kernel, (own, near, *weights), range(local, cut))
    near = run(more_kernel, (own, near, *weights), range(cut, count))
    parts = 2
    size = rows // parts
    back = [[] for _ in range(parts)]
    for a in range(1, chips):
        opened = run(near_kernel, (far[a - 1], *weights[:3]), range(local))
        for h in range(parts):
            s = kernel(
                functools.partial(far_kernel, range(local, count), h * size),
                shape((size, latent)), (far[a - 1], opened, *weights), [VM] * 8, 14,
                local * work // parts, local * load, [pltpu.VMEM((size, latent), F32)])
            back[h].append(swap(s, "expert", 2 * a))

    pair = kernel(join_kernel, shape((latent, chips * depth)), (own_up, *ups_x),
                  [VM] * chips, 4, 0, 4 * chips * depth * latent)
    ups = {(0, 0): pair}
    if far_z is not None:
        ups[(0, 1)] = swap(pair, "replica", 1)
        ups[(0, "A")] = swap_pair(pair, ("groups", "replica"), lambda i, j: (i, j ^ (2 + i)))
        ups[(0, "B")] = swap(ups[(0, "A")], "groups", 1)
    else:
        for b in range(1, spread):
            ups[(0, b)] = swap(pair, "replica", b)
    for _, b in list(ups):
        ups[(1, b)] = swap(ups[(0, b)], "expert", 1)
    order = list(ups)
    result = None
    for h in range(parts):
        operands = (near, *back[h], *[ups[k] for k in order])
        result = kernel(
            functools.partial(final_kernel, len(back[h]), h * size, order, spread, depth),
            shape((rows, width)), operands + ((result,) if h else ()),
            [VM] * len(operands) + [AN] * h, 10, 2 * size * width * latent, 2 * width * latent,
            [pltpu.VMEM((size, width), BF16), pltpu.SemaphoreType.DMA],
            AN, {len(operands): 0} if h else {})
    return result


def solution(mesh):
    placed = (
        P(("groups", "expert", "replica"), None),
        P(),
        P(),
        P(("expert", "replica"), None),
        P(("expert", "replica"), None),
        P("expert", None, None),
        P("expert", None, None),
        P("expert", None, None),
        P(("groups", "expert", "replica"), None),
        P(("groups", "expert", "replica"), None),
        P(("groups", "expert", "replica"), None, None, None),
    )

    return jax.shard_map(
        on_device,
        mesh=mesh,
        in_specs=placed,
        out_specs=P(("groups", "expert", "replica"), None),
        check_vma=False,
    )
```

```python
import functools

import jax
import jax.numpy as jnp
from jax import lax
from jax.experimental import pallas as pl
from jax.experimental.pallas import tpu as pltpu
from jax.sharding import PartitionSpec as P

epsilon = 1e-06
F32 = jnp.float32
BF16 = jnp.bfloat16

VM = pl.BlockSpec(memory_space=pltpu.VMEM)
AN = pl.BlockSpec(memory_space=pl.ANY)


def here(copies):
    e = lax.axis_index("expert")
    rep = lax.axis_index("replica") if copies > 1 else 0
    return lax.rem(e, 2), e // 2, rep, lax.axis_index("groups")


def in_hbm(x):
    return pltpu.with_memory_space_constraint(x, pltpu.HBM)


def swap(x, axis, bits):
    size = lax.axis_size(axis)
    return lax.ppermute(x, axis, [(i, i ^ bits) for i in range(size)])


def swap_pair(x, axes, move):
    sizes = [lax.axis_size(axis) for axis in axes]
    pairs = []
    for i in range(sizes[0]):
        for j in range(sizes[1]):
            p, q = move(i, j)
            pairs.append((i * sizes[1] + j, p * sizes[1] + q))
    return lax.ppermute(x, axes, pairs)


def kernel(body, out_shape, operands, specs, mib, flops=0, nbytes=0, scratch=(), out_specs=None,
           aliases={}):
    many = isinstance(out_shape, tuple)
    if out_specs is None:
        out_specs = (VM,) * len(out_shape) if many else VM
    return pl.pallas_call(
        body,
        out_shape=out_shape,
        in_specs=specs,
        out_specs=out_specs,
        scratch_shapes=list(scratch),
        input_output_aliases=aliases,
        compiler_params=pltpu.CompilerParams(vmem_limit_bytes=mib * 1024 * 1024),
        cost_estimate=pl.CostEstimate(flops=flops, bytes_accessed=nbytes, transcendentals=0),
    )(*operands)


def norm_kernel(tok_hbm, gain_hbm, *refs):
    n = (len(refs) - 4) // 2
    normed_ref, (tok_ref, gain_ref, sem) = refs[n], refs[-3:]
    pairs = ((tok_hbm, tok_ref), (gain_hbm, gain_ref), *zip(refs[:n], refs[n + 1:-3]))
    copies = [pltpu.make_async_copy(src, dst, sem.at[i]) for i, (src, dst) in enumerate(pairs)]
    for copy in copies:
        copy.start()
    for copy in copies[:2]:
        copy.wait()
    values = tok_ref[...].astype(F32)
    scale = lax.rsqrt(jnp.mean(values * values, axis=-1, keepdims=True) + epsilon)
    normed_ref[...] = (values * scale * gain_ref[...]).astype(BF16)
    for copy in copies[2:]:
        copy.wait()


def gate_kernel(top, normed_ref, router_ref, ids_ref, slot_ref, list_hbm, wt_ref, list_ref, sem):
    load = pltpu.make_async_copy(list_hbm, list_ref, sem)
    load.start()
    logits = lax.dot_general(router_ref[...], normed_ref[...], (((1,), (1,)), ((), ())),
                             preferred_element_type=F32)
    sig = jax.nn.sigmoid(logits)
    experts, rows = sig.shape
    sub = lax.broadcasted_iota(jnp.int32, (experts, rows), 0)
    lane = lax.broadcasted_iota(jnp.int32, (experts, rows), 1)
    total = jnp.zeros((experts, rows), F32)
    served = jnp.zeros((experts, rows), F32)
    for k in range(top):
        hit = sub == ids_ref[k:k + 1, :]
        total = total + jnp.where(hit, 1.0, 0.0)
        served = served + jnp.where(hit & (slot_ref[k:k + 1, :] >= 0), 1.0, 0.0)
    load.wait()
    _, shards, copies_n, local = list_ref.shape

    width = 128
    column = lax.broadcasted_iota(jnp.int32, (experts, width), 0)

    def listed(copy, served):
        owner = jnp.full((experts, width), -1, jnp.int32)
        for shard in range(shards):
            for m in range(local):
                entry = list_ref[0, shard, copy, m]
                row = jnp.where(entry >= 0, entry, -top) // top
                owner = jnp.where(column == shard * local + m, row, owner)
        hits = [jnp.where(lane[:, i:i + width] == owner, 1.0, 0.0) for i in range(0, rows, width)]
        return served + jnp.concatenate(hits, axis=1)

    served = lax.fori_loop(0, copies_n, listed, served)
    denom = jnp.sum(total * sig, axis=0, keepdims=True)
    wt_ref[...] = jnp.where(served > 0.0, sig / denom, 0.0)


def pile_kernel(*refs):
    depth = refs[0].shape[0]
    for i, x_ref in enumerate(refs[:-1]):
        refs[-1][i * depth:(i + 1) * depth, :] = x_ref[...]


def pick(chunks, other, depth, copies, normed_ref, x_ref):
    core, half, rep, group = here(copies)
    for i, (a, b) in enumerate(chunks):
        b = {"A": 2 + group, "B": 3 - group}.get(b, b)
        at = ((2 * (half ^ a) + (core ^ other)) * copies + (rep ^ b)) * depth
        x_ref[:, i * depth:(i + 1) * depth] = normed_ref[:, pl.ds(pl.multiple_of(at, depth), depth)]


def early_kernel(chunks, depth, copies, normed_ref, w0_ref, w1_ref, out_ref, x_ref):
    pick(chunks, 0, depth, copies, normed_ref, x_ref.at[0])
    pick(chunks, 1, depth, copies, normed_ref, x_ref.at[1])
    out_ref[...] = (jnp.dot(x_ref[0], w0_ref[...], preferred_element_type=F32)
                    + jnp.dot(x_ref[1], w1_ref[...], preferred_element_type=F32))


def late_kernel(chunks, copies, normed_ref, sum_ref, wt_ref, *refs):
    w_refs, (out_ref, x_ref, w_ref) = refs[:-3], refs[-3:]
    n = len(chunks)
    rows = normed_ref.shape[0]
    depth = w_refs[0].shape[0]
    for c in range(2):
        pick(chunks, c, depth, copies, normed_ref, x_ref.at[:, c * n * depth:(c + 1) * n * depth])
    for i, chunk in enumerate(w_refs):
        w_ref[i * depth:(i + 1) * depth, :] = chunk[...]
    out_ref[:rows, :] = (sum_ref[...] + jnp.dot(x_ref[...], w_ref[...],
                                                preferred_element_type=F32)).astype(BF16)
    wt = wt_ref[...]
    lead = wt.astype(BF16)
    out_ref[rows:, :rows] = lead
    out_ref[rows:, rows:] = (wt - lead.astype(F32)).astype(BF16)


def expert(x, weight, gate_w, up_w, down_w):
    gate = jnp.dot(x, gate_w, preferred_element_type=F32)
    upper = jnp.dot(x, up_w, preferred_element_type=F32)
    half = 0.5 * gate
    hidden = ((half + half * jnp.tanh(half)) * upper).astype(BF16)
    result = jnp.dot(hidden, down_w, preferred_element_type=F32).astype(BF16)
    return result.astype(F32) * weight


def columns(me, local, pay_ref, at, size):
    rows = pay_ref.shape[1] // 2
    wt = (pay_ref[rows:, at:at + size].astype(F32)
          + pay_ref[rows:, rows + at:rows + at + size].astype(F32))
    sub = lax.broadcasted_iota(jnp.int32, wt.shape, 0)
    picked = [jnp.sum(jnp.where(sub == (me ^ c) * local + j, wt, 0.0), axis=0, keepdims=True)
              for c in range(2) for j in range(local)]
    pad = [jnp.zeros((-len(picked) % 8, size), F32)] if len(picked) % 8 else []
    return jnp.concatenate(picked + pad, axis=0).T


def run_experts(span, at, size, pay_ref, w_refs, out_ref, start_ref=None):
    local = w_refs[0].shape[0]
    cols = columns(lax.axis_index("expert"), local, pay_ref, at, size)
    x = pay_ref[at:at + size, :]
    for j in span:
        refs = w_refs[:3] if j < local else w_refs[-3:]
        part = expert(x, cols[:, j:j + 1], *(ref[j % local] for ref in refs))
        if j == span[0]:
            out_ref[...] = part if start_ref is None else start_ref[at:at + size, :] + part
        else:
            out_ref[...] += part


def near_kernel(span, pay_ref, *refs):
    run_experts(span, 0, refs[-1].shape[0], pay_ref, refs[:-1], refs[-1])


def more_kernel(span, pay_ref, sum_ref, *refs):
    run_experts(span, 0, refs[-1].shape[0], pay_ref, refs[:-1], refs[-1], sum_ref)


def far_kernel(span, at, pay_ref, sum_ref, *refs):
    out_ref, acc_ref = refs[-2:]
    run_experts(span, at, out_ref.shape[0], pay_ref, refs[:6], acc_ref, sum_ref)
    out_ref[...] = acc_ref[...].astype(BF16)


def join_kernel(*refs):
    depth = refs[0].shape[0]
    for i, x_ref in enumerate(refs[:-1]):
        refs[-1][:, i * depth:(i + 1) * depth] = x_ref[...].T


def final_kernel(n_back, at, chunks, copies, depth, near_ref, *refs):
    out_ref, rows_ref, sem = refs[-3:]
    core, half, rep, group = here(copies)
    size = rows_ref.shape[0]
    total = near_ref[at:at + size, :]
    for s_ref in refs[:n_back]:
        total = total + s_ref[...].astype(F32)
    merged = total.astype(BF16)
    for (c, b), w_ref in zip(chunks, refs[n_back:]):
        b = {"A": 2 + group, "B": 3 - group}.get(b, b)
        block = jnp.dot(merged, w_ref[...], preferred_element_type=F32).astype(BF16)
        for a in range(w_ref.shape[1] // depth):
            e = 2 * (half ^ a) + (core ^ c)
            to = pl.multiple_of((e * copies + (rep ^ b)) * depth, depth)
            rows_ref[:, pl.ds(to, depth)] = block[:, a * depth:(a + 1) * depth]
    out = pltpu.make_async_copy(rows_ref, out_ref.at[pl.ds(at, size), :], sem)
    out.start()
    out.wait()


def shape(dims, dtype=BF16):
    return jax.ShapeDtypeStruct(dims, dtype)


def on_device(tokens, norm_gain, router, down_proj, up_proj, expert_gate, expert_up, expert_down,
              expert_ids, slot_pos, overflow_list):
    rows, width = tokens.shape
    top = expert_ids.shape[1]
    local, _, ff = expert_gate.shape
    depth, latent = down_proj.shape
    groups = lax.axis_size("groups")
    shards = lax.axis_size("expert")
    copies = lax.axis_size("replica")
    chips = shards // 2
    wide = copies * depth
    spread = copies
    if depth % 128:
        down_proj = lax.all_gather(down_proj, "replica", axis=0, tiled=True)
        up_proj = lax.all_gather(up_proj, "replica", axis=0, tiled=True)
        depth, spread = wide, 1
    experts = shards * local
    down = {(0, 0): down_proj}
    far_z = None
    if spread == groups + 2 and groups == 2:
        near_z = swap(down_proj, "replica", 1)
        far_z = swap_pair(down_proj, ("groups", "replica"), lambda i, j: (i, j ^ (2 + i)))
        down[(0, 1)] = near_z
        down[(0, "A")] = far_z
        for a in range(1, chips):
            down[(a, 0)] = swap(down_proj, "expert", 2 * a)
        ups_x = [swap(up_proj, "expert", 2 * a) for a in range(1, chips)]
        for a in range(1, chips):
            down[(a, 1)] = swap(down[(a, 0)], "replica", 1)
            down[(a, "B")] = swap_pair(far_z, ("groups", "expert"),
                                       lambda i, j: (i ^ 1, j ^ (2 * a)))
            down[(a, "A")] = swap(far_z, "expert", 2 * a)
        down[(0, "B")] = swap(far_z, "groups", 1)
    else:
        for b in range(1, spread):
            down[(0, b)] = swap(down_proj, "replica", b)
        for b in range(spread):
            for a in range(1, chips):
                down[(a, b)] = swap(down[(0, b)], "expert", 2 * a)
        ups_x = [swap(up_proj, "expert", 2 * a) for a in range(1, chips)]

    moved = (down_proj, up_proj, router.T, expert_ids.T, slot_pos.T)
    normed, own_down, own_up, *routing = kernel(
        norm_kernel, (shape((rows, width)), *[shape(x.shape, x.dtype) for x in moved]),
        tuple(map(in_hbm, (tokens, norm_gain.reshape(1, width), *moved))), [AN] * (2 + len(moved)), 18,
        8 * rows * width, 4 * rows * width,
        [pltpu.VMEM((rows, width), BF16), pltpu.VMEM((1, width), F32),
         pltpu.SemaphoreType.DMA((2 + len(moved),))])
    wt = kernel(
        functools.partial(gate_kernel, top), shape((experts, rows), F32),
        (normed, *routing, in_hbm(overflow_list)), [VM] * 4 + [AN], 10, 4 * rows * width * experts,
        2 * rows * width, [pltpu.SMEM(overflow_list.shape, jnp.int32), pltpu.SemaphoreType.DMA])
    down[(0, 0)] = own_down
    weights = (expert_gate, expert_up, expert_down, *[
        swap(w, "expert", 1) for w in (expert_gate, expert_up, expert_down)])

    late = [k for k in down if (k[1] == "A" and k[0]) or k[1] == "B"] or list(down)[-1:]
    early = [k for k in down if k not in late]

    n = len(early)
    stacked = kernel(pile_kernel, shape((n * depth, latent)), [down[k] for k in early], [VM] * n,
                     6, 0, 4 * n * depth * latent)
    stacked_core = swap(stacked, "expert", 1)
    late_core = [swap(down[k], "expert", 1) for k in late]
    opened = kernel(
        functools.partial(early_kernel, early, depth, spread), shape((rows, latent), F32),
        (normed, stacked, stacked_core), [VM] * 3, 10, 4 * rows * n * depth * latent,
        4 * n * depth * latent, [pltpu.VMEM((2, rows, n * depth), BF16)])
    n = len(late)
    own = kernel(
        functools.partial(late_kernel, late, spread), shape((rows + experts, latent)),
        (normed, opened, wt, *[down[k] for k in late], *late_core), [VM] * (3 + 2 * n), 10,
        4 * rows * n * depth * latent, 4 * n * depth * latent,
        [pltpu.VMEM((rows, 2 * n * depth), BF16), pltpu.VMEM((2 * n * depth, latent), BF16)])
    work = 6 * rows * latent * ff
    load = 6 * latent * ff
    count = 2 * local
    cut = count - local // 2
    far = [swap(own, "expert", 2 * a) for a in range(1, chips)]

    def run(body, operands, span):
        return kernel(
            functools.partial(body, span), shape((rows, latent), F32), operands, [VM] * len(operands),
            16, len(span) * work, len(span) * load)

    near = run(near_kernel, (own, *weights[:3]), range(local))
    near = run(more_kernel, (own, near, *weights), range(local, cut))
    near = run(more_kernel, (own, near, *weights), range(cut, count))
    parts = 2
    size = rows // parts
    back = [[] for _ in range(parts)]
    for a in range(1, chips):
        opened = run(near_kernel, (far[a - 1], *weights[:3]), range(local))
        for h in range(parts):
            s = kernel(
                functools.partial(far_kernel, range(local, count), h * size),
                shape((size, latent)), (far[a - 1], opened, *weights), [VM] * 8, 14,
                local * work // parts, local * load, [pltpu.VMEM((size, latent), F32)])
            back[h].append(swap(s, "expert", 2 * a))

    pair = kernel(join_kernel, shape((latent, chips * depth)), (own_up, *ups_x),
                  [VM] * chips, 4, 0, 4 * chips * depth * latent)
    ups = {(0, 0): pair}
    if far_z is not None:
        ups[(0, 1)] = swap(pair, "replica", 1)
        ups[(0, "A")] = swap_pair(pair, ("groups", "replica"), lambda i, j: (i, j ^ (2 + i)))
        ups[(0, "B")] = swap(ups[(0, "A")], "groups", 1)
    else:
        for b in range(1, spread):
            ups[(0, b)] = swap(pair, "replica", b)
    for _, b in list(ups):
        ups[(1, b)] = swap(ups[(0, b)], "expert", 1)
    order = list(ups)
    result = None
    for h in range(parts):
        operands = (near, *back[h], *[ups[k] for k in order])
        result = kernel(
            functools.partial(final_kernel, len(back[h]), h * size, order, spread, depth),
            shape((rows, width)), operands + ((result,) if h else ()),
            [VM] * len(operands) + [AN] * h, 10, 2 * size * width * latent, 2 * width * latent,
            [pltpu.VMEM((size, width), BF16), pltpu.SemaphoreType.DMA],
            AN, {len(operands): 0} if h else {})
    return result


def solution(mesh):
    placed = (
        P(("groups", "expert", "replica"), None),
        P(),
        P(),
        P(("expert", "replica"), None),
        P(("expert", "replica"), None),
        P("expert", None, None),
        P("expert", None, None),
        P("expert", None, None),
        P(("groups", "expert", "replica"), None),
        P(("groups", "expert", "replica"), None),
        P(("groups", "expert", "replica"), None, None, None),
    )

    return jax.shard_map(
        on_device,
        mesh=mesh,
        in_specs=placed,
        out_specs=P(("groups", "expert", "replica"), None),
        check_vma=False,
    )
```
